32 devices in a mesh: dp: 16 (over z, y, x), mp: 2 (over core).
Axes of the slice: x: 2, y: 2, z: 4, core: 2. Of those that a mesh axis runs over, the one named last changes fastest.
Arguments:
- prompt_hidden: float32 [2048, 5120], P('dp'), may hold values from -6 to 6
- key_weight: float32 [5120, 1024], P('dp', 'mp'), may hold values from -0.078125 to 0.078125
- value_weight: float32 [5120, 1024], P('dp', 'mp'), may hold values from -0.078125 to 0.078125
- queries: float32 [4096, 5120], P('dp', 'mp'), may hold values from -21 to 21
- keys_resp: float32 [4096, 1024], P('dp', 'mp'), may hold values from -21 to 21
- response_value_rows: float32 [4096, 1024], P('dp', 'mp'), may hold values from -6 to 6
- grad_out: float32 [4096, 5120], P('dp', 'mp'), may hold values from -6 to 6
- resp_prompt: int32 [16], P('dp'), may hold values from 0 to 15, as said below
- resp_len: int32 [16], P('dp'), may hold values from 2 to 256
Outputs:
- attn_out: float32 [4096, 5120], P('dp', 'mp')
- grad_queries: float32 [4096, 5120], P('dp', 'mp')
- grad_keys_resp: float32 [4096, 1024], P('dp', 'mp')
- grad_values_resp: float32 [4096, 1024], P('dp', 'mp')
- grad_hidden: float32 [2048, 5120], P('dp', 'mp')
- grad_w_key: float32 [5120, 1024], P('dp', 'mp')
- grad_w_value: float32 [5120, 1024], P('dp', 'mp')
The draws below stay inside these ranges and needn't reach their ends.
Inputs may be any that keep to these rules, and one draw needn't show every extreme that they name: `resp_prompt`: every one of the 16 prompts has exactly 1 responses.
All inputs are finite; a program needn't handle non-finite values.
Results may differ from the reference program's by a relative error of at most 0.0003.
Values sent between devices are 32-bit elements; how exact they have to be, the bound alone decides.
No kernel may reach another device: no remote copies, remote signals or barrier semaphores. Data moves between devices by JAX's collectives and lax.ppermute only.
A program may use at most 192 MiB of HBM per device.

```python
import math
import jax
import jax.numpy as jnp
from jax import lax

MODEL_WIDTH = 5120
QUERY_HEADS = 40
KEY_VALUE_HEADS = 8
HEAD_SIZE = 128
PROMPT_COUNT = 16
RESPONSE_LENGTH = 256
RESPONSE_COUNT = 16
RESPONSE_TOKENS = 4096
PROMPT_ROWS = 2048
PROMPT_LENGTH = 128


def draw_queries(key, part):
    queries_per_group = QUERY_HEADS // KEY_VALUE_HEADS
    value_rows = jnp.clip(jax.random.normal(jax.random.fold_in(key, 11), (RESPONSE_COUNT, RESPONSE_LENGTH, KEY_VALUE_HEADS, queries_per_group, HEAD_SIZE), jnp.float32), -4.0, 4.0)
    return value_rows.reshape(RESPONSE_COUNT * RESPONSE_LENGTH, QUERY_HEADS * HEAD_SIZE)


def draw_keys_resp(key, part):
    value_rows = jnp.clip(jax.random.normal(jax.random.fold_in(key, 12), (RESPONSE_COUNT, RESPONSE_LENGTH, KEY_VALUE_HEADS, HEAD_SIZE), jnp.float32), -4.0, 4.0)
    return value_rows.reshape(RESPONSE_COUNT * RESPONSE_LENGTH, KEY_VALUE_HEADS * HEAD_SIZE)


def draw_resp_prompt(key, part):
    listing = jnp.arange(RESPONSE_COUNT, dtype=jnp.int32) % PROMPT_COUNT
    return jax.random.permutation(jax.random.fold_in(key, 21), listing).astype(jnp.int32)


def draw_resp_len(key, part):
    lengths = jax.random.randint(jax.random.fold_in(key, 31), (RESPONSE_COUNT,), 2, RESPONSE_LENGTH + 1, dtype=jnp.int32)
    where_full = jax.random.randint(jax.random.fold_in(key, 32), (), 0, RESPONSE_COUNT, dtype=jnp.int32)
    return lengths.at[where_full].set(RESPONSE_LENGTH)


def level_of(stream_key, extent, shards, least, top_value):
    loudness, own = 1.0, jax.random.fold_in(stream_key, 6)
    for dim, blocks in shards:
        heights = jnp.exp(jax.random.uniform(jax.random.fold_in(own, dim), (blocks,), jnp.float32, least / len(shards), top_value / len(shards)))
        loudness = loudness * jnp.repeat(heights, extent[dim] // blocks).reshape([-1 if axis == dim else 1 for axis in range(len(extent))])
    return loudness


def centred(own_key, shape, scale, reach, cuts=(), held_as=jnp.bfloat16):
    values = scale * jax.random.normal(own_key, shape, jnp.float32)
    if cuts:
        values = values * level_of(own_key, shape, cuts, -0.22, 0.18)
    return jnp.clip(values, -reach, reach).astype(held_as)


def setup_inputs(seed: int = 0) -> dict:
    key_of = jax.random.split(jax.random.key(seed), 10)
    prompt_hidden = centred(key_of[0], (PROMPT_ROWS, MODEL_WIDTH), 1.0, 6.0, ((0, 16),), jnp.float32)
    key_weight = centred(key_of[1], (MODEL_WIDTH, KEY_VALUE_HEADS * HEAD_SIZE), MODEL_WIDTH ** -0.5, 0.078125, ((0, 16), (1, 2)), jnp.float32)
    value_weight = centred(key_of[2], (MODEL_WIDTH, KEY_VALUE_HEADS * HEAD_SIZE), MODEL_WIDTH ** -0.5, 0.078125, ((0, 16), (1, 2)), jnp.float32)
    queries = draw_queries(jax.random.fold_in(key_of[9], 71), 0)
    keys_resp = draw_keys_resp(jax.random.fold_in(key_of[9], 71), 0)
    response_value_rows = centred(key_of[5], (RESPONSE_TOKENS, KEY_VALUE_HEADS * HEAD_SIZE), 1.0, 6.0, ((0, 16), (1, 2)), jnp.float32)
    grad_out = centred(key_of[6], (RESPONSE_TOKENS, QUERY_HEADS * HEAD_SIZE), 1.0, 6.0, ((0, 16), (1, 2)), jnp.float32)
    resp_prompt = draw_resp_prompt(jax.random.fold_in(key_of[9], 71), 0)
    resp_len = draw_resp_len(jax.random.fold_in(key_of[9], 71), 0)
    return dict(prompt_hidden=prompt_hidden, key_weight=key_weight, value_weight=value_weight, queries=queries, keys_resp=keys_resp, response_value_rows=response_value_rows, grad_out=grad_out, resp_prompt=resp_prompt, resp_len=resp_len)


masked_value = -1e+30

def reference(prompt_hidden, key_weight, value_weight, queries, keys_resp, response_value_rows, grad_out, resp_prompt, resp_len):
    highest_precision = lax.Precision.HIGHEST
    queries_per_group = QUERY_HEADS // KEY_VALUE_HEADS
    score_scale = 1.0 / math.sqrt(HEAD_SIZE)

    def forward(hidden_input, key_matrix, value_matrix, combined_queries, combined_keys, combined_values):
        prompt_key_rows = jnp.dot(hidden_input, key_matrix, precision=highest_precision, preferred_element_type=jnp.float32).reshape(PROMPT_COUNT, PROMPT_LENGTH, KEY_VALUE_HEADS, HEAD_SIZE)
        prompt_value_rows = jnp.dot(hidden_input, value_matrix, precision=highest_precision, preferred_element_type=jnp.float32).reshape(PROMPT_COUNT, PROMPT_LENGTH, KEY_VALUE_HEADS, HEAD_SIZE)
        response_queries = combined_queries.reshape(RESPONSE_COUNT, RESPONSE_LENGTH, KEY_VALUE_HEADS, queries_per_group, HEAD_SIZE)
        response_keys = combined_keys.reshape(RESPONSE_COUNT, RESPONSE_LENGTH, KEY_VALUE_HEADS, HEAD_SIZE)
        response_values = combined_values.reshape(RESPONSE_COUNT, RESPONSE_LENGTH, KEY_VALUE_HEADS, HEAD_SIZE)

        def single(items):
            query, key_own, value_own, prompt, length = items
            key_cat = jnp.concatenate([prompt_key_rows[prompt], key_own], 0)
            value_cat = jnp.concatenate([prompt_value_rows[prompt], value_own], 0)
            scores = jnp.einsum('igqd,jgd->gqij', query, key_cat, precision=highest_precision) * score_scale
            rows = jnp.arange(RESPONSE_LENGTH, dtype=jnp.int32)[:, None]
            cols = jnp.arange(PROMPT_LENGTH + RESPONSE_LENGTH, dtype=jnp.int32)[None, :]
            offset = cols - PROMPT_LENGTH
            allowed = (cols < PROMPT_LENGTH) | (offset <= rows) & (offset < length)
            scores = jnp.where(allowed[None, None], scores, masked_value)
            top = lax.optimization_barrier(jnp.max(scores, axis=-1, keepdims=True))
            expo = jnp.exp(scores - top)
            attn_prob = expo / lax.optimization_barrier(jnp.sum(expo, axis=-1, keepdims=True))
            result = jnp.einsum('gqij,jgd->igqd', attn_prob, value_cat, precision=highest_precision)
            valid = (jnp.arange(RESPONSE_LENGTH, dtype=jnp.int32) < length)[:, None, None, None]
            return jnp.where(valid, result, 0.0)
        single = jax.checkpoint(single)
        outputs = lax.map(single, (response_queries, response_keys, response_values, resp_prompt, resp_len))
        return outputs.reshape(RESPONSE_COUNT * RESPONSE_LENGTH, QUERY_HEADS * HEAD_SIZE)
    attn_out, pullback = jax.vjp(forward, prompt_hidden, key_weight, value_weight, queries, keys_resp, response_value_rows)
    grads = pullback(grad_out)
    return (attn_out, grads[3], grads[4], grads[5], grads[0], grads[1], grads[2])
```

```python
import functools
import math

import jax
import jax.numpy as jnp
from jax import lax
from jax.experimental import pallas as pl
from jax.experimental.pallas import tpu as pltpu
from jax.sharding import PartitionSpec as P

QUERY_HEADS = 40
KEY_VALUE_HEADS = 8
HEAD_SIZE = 128
PROMPT_COUNT = 16
RESPONSE_LENGTH = 256

masked_value = -1e30
HIGH = lax.Precision.HIGH
BOTH = ("dp", "mp")


def pairs_of(target):
    return [
        (c * 2 + m, target(c, m) * 2 + m)
        for c in range(16)
        for m in range(2)
        if target(c, m) is not None
    ]


def along_z(moves):
    return pairs_of(lambda c, m: moves[c >> 2] << 2 | c & 3 if c >> 2 in moves else None)


SECOND = pairs_of(lambda c, m: c ^ (2, 1)[m])
THIRD = pairs_of(lambda c, m: c ^ (1, 2)[m])
ACROSS = [along_z({z: z ^ k for z in range(4)}) for k in range(4)]
MIDDLE = along_z({1: 2, 2: 1})
INWARD = along_z({0: 1, 3: 2})
OUTWARD = along_z({1: 0, 2: 3})
SWAP = [(0, 1), (1, 0)]


def permute(x, pairs):
    return lax.ppermute(x, BOTH, pairs)


def spread(block):
    second = permute(block, SECOND)
    return [block, second, permute(block, THIRD), permute(second, THIRD)]


def gather_blocks(block):
    out = spread(block)
    for k in range(1, 4):
        out += spread(permute(block, ACROSS[k]))
    return out


def gathered_order(chip, core):
    inner = jnp.where(core == 0, jnp.array([0, 2, 1, 3]), jnp.array([0, 1, 2, 3]))
    return (chip ^ (jnp.arange(4)[:, None] * 4) ^ inner[None, :]).reshape(16)


def scatter_order(chip, core):
    z = chip // 4
    rows = jnp.array([[3, 2, 1, 0], [3, 2, 0, 1], [0, 1, 3, 2], [0, 1, 2, 3]])
    z_order = jnp.sum(jnp.where(jnp.arange(4)[:, None] == z, rows, 0), 0)
    inner = jnp.where(core == 0, jnp.array([3, 1, 2, 0]), jnp.array([3, 2, 1, 0]))
    return (z_order[:, None] * 4 + ((chip & 3) ^ inner)[None, :]).reshape(16)


def reduce_blocks(send, keep):
    part = []
    for k in range(4):
        rows = keep[k].shape[0] // 2
        come = permute(send[k], THIRD)
        passing = keep[k][:rows] + come[:rows]
        part.append(keep[k][rows:] + come[rows:] + permute(passing, SECOND))
    first = permute(part[0], INWARD)
    second = permute(part[1], INWARD)
    third = permute(part[2], INWARD)
    passed = permute(part[0] + first, MIDDLE)
    later = permute(part[1] + second, MIDDLE)
    last = permute(part[2] + passed, OUTWARD)
    return part[3] + third + later + last


def two_terms(x):
    upper = x.astype(jnp.bfloat16)
    return upper, (x - upper.astype(jnp.float32)).astype(jnp.bfloat16)


def dot(a, b, dims):
    return lax.dot_general(a, b, (dims, ((), ())), preferred_element_type=jnp.float32)


def dot_terms(a, b, dims=((1,), (0,))):
    return dot(a[0], b[0], dims) + (dot(a[0], b[1], dims) + dot(a[1], b[0], dims))


def dot_rows(a, b):
    dims = ((1,), (1,))
    return dot(jnp.concatenate(a, 1), jnp.concatenate([b[0], b[0]], 1), dims) + dot(a[0], b[1], dims)


def three_terms(x):
    first = x.astype(jnp.bfloat16)
    rest = x - first.astype(jnp.float32)
    second = rest.astype(jnp.bfloat16)
    return first, second, (rest - second.astype(jnp.float32)).astype(jnp.bfloat16)


def dot_rows_exact(a, b):
    a, b = three_terms(a), three_terms(b)
    dims = ((1,), (1,))
    pair = jnp.concatenate(a[:2], 1)
    small = dot(jnp.concatenate([a[2], a[0]], 1), jnp.concatenate([b[0], b[2]], 1), dims)
    small = small + dot(pair, jnp.concatenate([b[1], b[1]], 1), dims)
    return dot(pair, jnp.concatenate([b[0], b[0]], 1), dims) + small


VMEM_LIMIT = 56 << 20


def call(kernel, name, grid, in_specs, out_specs, out_shape, scalars=0, scratch=()):
    return pl.pallas_call(
        kernel,
        out_shape=[jax.ShapeDtypeStruct(*shape) for shape in out_shape],
        grid_spec=pltpu.PrefetchScalarGridSpec(
            num_scalar_prefetch=scalars,
            grid=grid,
            in_specs=in_specs,
            out_specs=out_specs,
            scratch_shapes=scratch,
        ),
        compiler_params=pltpu.CompilerParams(vmem_limit_bytes=VMEM_LIMIT),
        name=name,
    )


def whole(x):
    return pl.BlockSpec(x.shape, lambda *_: (0,) * x.ndim)


def turn_kernel(core, x, out):
    t = x[...].T
    count, half, _ = out.shape
    for c in range(count):
        own = t[2 * c * half : 2 * (c + 1) * half]
        out[c] = jnp.where(core[0] == 0, own[:half], own[half:])


def turn(core, hidden, chips):
    rows, model = hidden.shape
    half = model // chips // 2
    (out,) = call(
        turn_kernel,
        "turn",
        (chips // 2,),
        [pl.BlockSpec((rows, model // chips * 2), lambda i, *_: (0, i))],
        [pl.BlockSpec((2, half, rows), lambda i, *_: (i, 0, 0))],
        [((chips, half, rows), jnp.float32)],
        scalars=1,
    )(core, hidden)
    return out


def turn_back_kernel(core, own, other, out):
    first = core[0] == 0
    parts = []
    for c in range(own.shape[0]):
        x, y = own[c], other[c]
        parts += [jnp.where(first, x, y), jnp.where(first, y, x)]
    out[...] = jnp.concatenate(parts, 0).T


def turn_back(core, back, come):
    chips, half, rows = back.shape
    steps = chips // 4
    (out,) = call(
        turn_back_kernel,
        "turn_back",
        (steps,),
        [
            pl.BlockSpec((2, half, rows), lambda i, core: (core[0] * steps + i, 0, 0)),
            pl.BlockSpec((2, half, rows), lambda i, core: (i, 0, 0)),
        ],
        [pl.BlockSpec((rows, 4 * half), lambda i, *_: (0, i))],
        [((rows, chips * half), jnp.float32)],
        scalars=1,
    )(core, back, come)
    return out


def split_kernel(core, key, value, upper, lower):
    half = key.shape[0] // 2
    first = core[0] == 0
    for start, ref in ((0, key), (key.shape[1], value)):
        x, y = ref[:half], ref[half:]
        for row, part in ((0, jnp.where(first, x, y)), (half, jnp.where(first, y, x))):
            terms = two_terms(part)
            for out, term in ((upper, terms[0]), (lower, terms[1])):
                out[row : row + half, start : start + key.shape[1]] = term


def split_weights(core, key, value):
    shape = ((key.shape[0], 2 * key.shape[1]), jnp.bfloat16)
    out = pl.BlockSpec(shape[0], lambda *_: (0, 0))
    return call(
        split_kernel, "split_weights", (1,), [whole(key), whole(value)], [out] * 2, [shape] * 2, scalars=1
    )(core, key, value)


def project_kernel(index, *refs):
    own, other, (upper, lower), outs = refs[:4], refs[4:8], refs[8:10], refs[10:]
    x = jnp.concatenate(
        [
            jnp.concatenate([ref[0] for ref in own], 1),
            jnp.concatenate([ref[0] for ref in other], 1),
        ],
        0,
    )
    terms = dot_terms(two_terms(x), (upper[...], lower[...]), ((0,), (0,)))
    count = outs[0].shape[0]
    outs[0][...] = terms[:count]
    outs[1][...] = terms[count:]


def project(index, own, other, weight_terms):
    _, half, plen = own.shape
    columns = weight_terms[0].shape[1]
    picked = [
        pl.BlockSpec((1, half, plen), lambda i, index, q=q: (index[q], 0, 0)) for q in range(4)
    ]
    shape = ((2 * plen, columns), jnp.float32)
    return call(
        project_kernel,
        "project",
        (1,),
        picked * 2 + [whole(weight_terms[0])] * 2,
        [pl.BlockSpec(shape[0], lambda *_: (0, 0))] * 2,
        [shape] * 2,
        scalars=1,
    )(index, *([own] * 4), *([other] * 4), *weight_terms)


def hidden_grad_kernel(listed, *refs):
    blocks, (upper, lower), (keep, give) = refs[:-4], refs[-4:-2], refs[-2:]
    half, plen = keep.shape[1:]
    weights = upper[...], lower[...]
    for q in range(0, len(blocks), 2):
        x = two_terms(jnp.concatenate([blocks[q][...], blocks[q + 1][...]], 0))
        terms = dot_terms(weights, x, ((1,), (1,)))
        for i in range(2):
            part = terms[:, i * plen : (i + 1) * plen]
            keep[listed[q + i]] = part[:half]
            give[listed[q + i]] = part[half:]


def hidden_grad(listed, blocks, weight_terms):
    plen, columns = blocks[0].shape
    count, half = len(blocks), weight_terms[0].shape[0] // 2
    shape = ((count, half, plen), jnp.float32)
    return call(
        hidden_grad_kernel,
        "hidden_grad",
        (1,),
        [whole(blocks[0])] * count + [whole(weight_terms[0])] * 2,
        [pl.BlockSpec(shape[0], lambda *_: (0, 0, 0))] * 2,
        [shape] * 2,
        scalars=1,
    )(listed, *blocks, *weight_terms)


def weight_grad_kernel(listed, core, own, other, *refs):
    blocks, outs = refs[:-2], refs[-2:]
    half = own.shape[1]
    width = outs[0].shape[1]
    total = None
    for q in range(0, len(blocks), 4):
        x = jnp.concatenate(
            [jnp.concatenate([ref[listed[q + i]] for i in range(4)], 1) for ref in (own, other)], 0
        )
        g = jnp.concatenate([ref[...] for ref in blocks[q : q + 4]], 0)
        term = dot_terms(two_terms(x), two_terms(g))
        total = term if total is None else total + term
    x, y = total[:half], total[half:]
    first = core[0] == 0
    for row, part in ((0, jnp.where(first, x, y)), (half, jnp.where(first, y, x))):
        for out, start in zip(outs, (0, width)):
            out[row : row + half] = part[:, start : start + width]


def weight_grad(listed, core, own, other, blocks):
    plen, columns = blocks[0].shape
    shape = ((2 * own.shape[1], columns // 2), jnp.float32)
    return call(
        weight_grad_kernel,
        "weight_grad",
        (1,),
        [whole(own)] * 2 + [whole(blocks[0])] * len(blocks),
        [pl.BlockSpec(shape[0], lambda *_: (0, 0))] * 2,
        [shape] * 2,
        scalars=2,
    )(listed, core, own, other, *blocks)


SCALE = 1.0 / math.sqrt(HEAD_SIZE)
PER_GROUP = QUERY_HEADS // KEY_VALUE_HEADS


def stack(ref):
    size = ref.shape[1] // PER_GROUP
    return jnp.concatenate([ref[:, h * size : (h + 1) * size] for h in range(PER_GROUP)], 0)


def unstack(ref, x):
    rows, size = ref.shape[0], ref.shape[1] // PER_GROUP
    for h in range(PER_GROUP):
        ref[:, h * size : (h + 1) * size] = x[h * rows : (h + 1) * rows]


def save_columns(ref, first, second):
    rows = ref.shape[0]
    lane = lax.broadcasted_iota(jnp.int32, ref.shape, 1)
    out = jnp.zeros(ref.shape, jnp.float32)
    for start, column in ((0, first), (8, second)):
        for h in range(PER_GROUP):
            out = jnp.where(lane == start + h, column[h * rows : (h + 1) * rows], out)
    ref[...] = out


def load_column(ref, start):
    return jnp.concatenate([ref[:, start + h : start + h + 1] for h in range(PER_GROUP)], 0)


def row_number(shape, rows):
    return lax.broadcasted_iota(jnp.int32, shape, 0) % rows


def own_scores(length, query, keys, rows):
    scores = dot_rows_exact(query, keys) * SCALE
    j = lax.broadcasted_iota(jnp.int32, scores.shape, 1)
    return jnp.where((j <= row_number(scores.shape, rows)) & (j < length), scores, masked_value)


def open_kernel(length, q, k, v, total, stats):
    scores = own_scores(length[0], stack(q), k[...], q.shape[0])
    top = jnp.max(scores, -1, keepdims=True)
    expo = jnp.exp(scores - top)
    unstack(total, dot_terms(two_terms(expo), two_terms(v[...])))
    save_columns(stats, top, jnp.sum(expo, -1, keepdims=True))


def close_kernel(length, q, g, kp, vp, total, stats, out, grad_scores, stats_out, gk, gv):
    query, keys, values = stack(q), kp[...], vp[...]
    scores = dot_rows_exact(query, keys) * SCALE
    before = load_column(stats, 0)
    top = jnp.maximum(before, jnp.max(scores, -1, keepdims=True))
    weight = jnp.exp(before - top)
    expo = jnp.exp(scores - top)
    denominator = weight * load_column(stats, 8) + jnp.sum(expo, -1, keepdims=True)
    inverse = 1.0 / denominator
    prob = expo * inverse
    prob_terms, value_terms = two_terms(prob), two_terms(values)
    result = (weight * inverse) * stack(total) + dot_terms(prob_terms, value_terms)
    valid = row_number(result.shape, q.shape[0]) < length[0]
    result = jnp.where(valid, result, 0.0)
    upstream = jnp.where(valid, stack(g), 0.0)
    upstream_terms = two_terms(upstream)
    inner = jnp.sum(upstream * result, -1, keepdims=True)
    grad = prob * (dot_rows(upstream_terms, value_terms) - inner) * SCALE
    unstack(out, result)
    unstack(grad_scores, grad)
    save_columns(stats_out, top + jnp.log(denominator), inner)
    gk[...] = dot_terms(two_terms(grad), two_terms(query), ((0,), (0,)))
    gv[...] = dot_terms(prob_terms, upstream_terms, ((0,), (0,)))


def finish_kernel(length, q, g, k, v, kp, grad_scores, stats, gq, gk, gv):
    query, keys = stack(q), k[...]
    rows = q.shape[0]
    prob = jnp.exp(own_scores(length[0], query, keys, rows) - load_column(stats, 0))
    upstream = stack(g)
    upstream = jnp.where(row_number(upstream.shape, rows) < length[0], upstream, 0.0)
    upstream_terms = two_terms(upstream)
    grad = prob * (dot_rows(upstream_terms, two_terms(v[...])) - load_column(stats, 8)) * SCALE
    grad_terms = two_terms(grad)
    prompt_part = dot_terms(two_terms(stack(grad_scores)), two_terms(kp[...]))
    unstack(gq, prompt_part + dot_terms(grad_terms, two_terms(keys)))
    gk[...] = dot_terms(grad_terms, two_terms(query), ((0,), (0,)))
    gv[...] = dot_terms(two_terms(prob), upstream_terms, ((0,), (0,)))


def attention(kernel, name, groups, length, ins, outs):
    return call(
        kernel,
        name,
        (groups,),
        [
            pl.BlockSpec((x.shape[0], size), lambda i, *_, skip=skip: (0, skip + i))
            for x, size, skip in ins
        ],
        [pl.BlockSpec(shape, lambda i, *_: (0, i)) for shape in outs],
        [((rows, groups * size), jnp.float32) for rows, size in outs],
        scalars=1,
    )(length, *(x for x, _, _ in ins))


def take_blocks(x, index):
    return jnp.stack(
        [lax.dynamic_index_in_dim(x, index[j], keepdims=False) for j in range(index.shape[0])]
    )


def take_small(table, index):
    hit = index[..., None] == jnp.arange(table.shape[0])
    return jnp.sum(jnp.where(hit, table, 0), -1)


def per_device(
    short,
    prompt_hidden,
    key_weight,
    value_weight,
    queries,
    keys_resp,
    response_value_rows,
    grad_out,
    resp_prompt,
    resp_len,
):
    chips = lax.axis_size("dp")
    chip, core = lax.axis_index("dp"), lax.axis_index("mp")
    rows_own, model = prompt_hidden.shape
    slice_width = model // chips
    width = key_weight.shape[1]
    groups = width // HEAD_SIZE
    plen = rows_own * chips // PROMPT_COUNT
    tokens = queries.shape[0]
    responses = tokens * chips // RESPONSE_LENGTH
    assert tokens == RESPONSE_LENGTH
    short = short and responses == PROMPT_COUNT
    here = core.astype(jnp.int32)[None]
    wide = PER_GROUP * HEAD_SIZE

    if short:
        all_prompts = jnp.where(jnp.arange(chips) == chip, resp_prompt, 0)
        for pairs in (ACROSS[1], ACROSS[2], SECOND, THIRD):
            all_prompts = all_prompts + permute(all_prompts, pairs)
        mine = lax.all_to_all(turn(here, prompt_hidden, chips), "dp", 0, 0)
        weight_terms = split_weights(here, key_weight, value_weight)
    else:
        all_prompts = lax.all_gather(resp_prompt, "dp", axis=0, tiled=True)
        hidden = lax.all_to_all(
            prompt_hidden.reshape(rows_own, chips, slice_width).transpose(1, 0, 2), "dp", 0, 0
        )
        hidden = hidden.reshape(PROMPT_COUNT, plen, slice_width)
        weights = jnp.concatenate([key_weight, value_weight], 1)

    q = (queries, wide, 0)
    total, stats = attention(
        open_kernel,
        "open",
        groups,
        resp_len,
        [q, (keys_resp, HEAD_SIZE, 0), (response_value_rows, HEAD_SIZE, 0)],
        [(tokens, wide), (tokens, HEAD_SIZE)],
    )

    if short:
        mine, weight_terms, total, stats, all_prompts = lax.optimization_barrier(
            (mine, weight_terms, total, stats, all_prompts)
        )
        other = lax.ppermute(mine, "mp", SWAP)
        listed = take_small(all_prompts, scatter_order(chip, core))
        pairs = [project(listed[4 * k : 4 * k + 4], mine, other, weight_terms) for k in range(4)]
        prompt_rows = reduce_blocks([pair[0] for pair in pairs], [pair[1] for pair in pairs])
    else:
        terms = jnp.einsum("rtc,ck->rtk", take_blocks(hidden, all_prompts), weights, precision=HIGH)
        prompt_rows = lax.psum_scatter(
            terms.reshape(responses * plen, 2 * width), "dp", scatter_dimension=0, tiled=True
        )

    g = (grad_out, wide, 0)
    prompt_keys = (prompt_rows, HEAD_SIZE, 0)
    result, grad_scores, stats, own_k, own_v = attention(
        close_kernel,
        "close",
        groups,
        resp_len,
        [q, g, prompt_keys, (prompt_rows, HEAD_SIZE, groups), (total, wide, 0), (stats, HEAD_SIZE, 0)],
        [(tokens, wide), (tokens, PER_GROUP * plen), (tokens, HEAD_SIZE)] + [(plen, HEAD_SIZE)] * 2,
    )
    grad_query, grad_keys, grad_values = attention(
        finish_kernel,
        "finish",
        groups,
        resp_len,
        [q, g, (keys_resp, HEAD_SIZE, 0), (response_value_rows, HEAD_SIZE, 0), prompt_keys]
        + [(grad_scores, PER_GROUP * plen, 0), (stats, HEAD_SIZE, 0)],
        [(tokens, wide)] + [(tokens, HEAD_SIZE)] * 2,
    )

    own = jnp.concatenate([own_k, own_v], 1)
    if short:
        gathered = gather_blocks(own)
        gathered, grad_query, grad_keys, grad_values = lax.optimization_barrier(
            (gathered, grad_query, grad_keys, grad_values)
        )
        listed = take_small(all_prompts, gathered_order(chip, core))
        keep, give = hidden_grad(listed, gathered, weight_terms)
        back = lax.all_to_all(keep + lax.ppermute(give, "mp", SWAP), "dp", 0, 0)
        grad_w_key, grad_w_value = weight_grad(listed, here, mine, other, gathered)
        back, grad_w_key, grad_w_value = lax.optimization_barrier((back, grad_w_key, grad_w_value))
        leave = jnp.where(core == 0, back[chips // 2 :], back[: chips // 2])
        grad_hidden = turn_back(here, back, lax.ppermute(leave, "mp", SWAP))
    else:
        gathered = lax.all_gather(own, "dp", axis=0, tiled=True).reshape(responses, plen, 2 * width)
        summed = jnp.einsum(
            "rtc,rtk->ck", take_blocks(hidden, all_prompts), gathered, precision=HIGH
        )
        grad_w_key, grad_w_value = summed[:, :width], summed[:, width:]
        terms = jnp.einsum("rtk,ck->rtc", gathered, weights, precision=HIGH)
        numbers = jnp.arange(responses)
        same = all_prompts[:, None] == all_prompts[None, :]
        earlier = jnp.sum(same & (numbers[None, :] < numbers[:, None]), 1)
        hidden_terms = 0.0
        for i in range(responses // PROMPT_COUNT):
            hit = (all_prompts[None, :] == jnp.arange(PROMPT_COUNT)[:, None]) & (earlier[None, :] == i)
            place = jnp.sum(jnp.where(hit, numbers[None, :], 0), -1)
            hidden_terms = hidden_terms + take_blocks(terms, place)
        back = lax.all_to_all(hidden_terms.reshape(chips, rows_own, slice_width), "dp", 0, 0)
        back = back.transpose(1, 0, 2).reshape(rows_own, model)
        grad_hidden = lax.psum_scatter(back, "mp", scatter_dimension=1, tiled=True)
    return (
        result,
        grad_query,
        grad_keys,
        grad_values,
        grad_hidden,
        grad_w_key,
        grad_w_value,
    )


def solution(mesh):
    short = mesh.shape["dp"] == 16 and mesh.shape["mp"] == 2
    in_specs = (P("dp", None),) + (P("dp", "mp"),) * 6 + (P("dp"),) * 2
    out_specs = (P("dp", "mp"),) * 7
    return jax.shard_map(
        functools.partial(per_device, short),
        mesh=mesh,
        in_specs=in_specs,
        out_specs=out_specs,
        check_vma=False,
    )
```

```python
import functools
import math

import jax
import jax.numpy as jnp
from jax import lax
from jax.experimental import pallas as pl
from jax.experimental.pallas import tpu as pltpu
from jax.sharding import PartitionSpec as P

QUERY_HEADS = 40
KEY_VALUE_HEADS = 8
HEAD_SIZE = 128
PROMPT_COUNT = 16
RESPONSE_LENGTH = 256

masked_value = -1e30
HIGH = lax.Precision.HIGH
BOTH = ("dp", "mp")


def pairs_of(target):
    return [
        (c * 2 + m, target(c, m) * 2 + m)
        for c in range(16)
        for m in range(2)
        if target(c, m) is not None
    ]


def along_z(moves):
    return pairs_of(lambda c, m: moves[c >> 2] << 2 | c & 3 if c >> 2 in moves else None)


SECOND = pairs_of(lambda c, m: c ^ (2, 1)[m])
THIRD = pairs_of(lambda c, m: c ^ (1, 2)[m])
ACROSS = [along_z({z: z ^ k for z in range(4)}) for k in range(4)]
MIDDLE = along_z({1: 2, 2: 1})
INWARD = along_z({0: 1, 3: 2})
OUTWARD = along_z({1: 0, 2: 3})
SWAP = [(0, 1), (1, 0)]


def permute(x, pairs):
    return lax.ppermute(x, BOTH, pairs)


def gathered_order(chip, core):
    inner = jnp.where(core == 0, jnp.array([0, 2, 1, 3]), jnp.array([0, 1, 2, 3]))
    return (chip ^ (jnp.arange(4)[:, None] * 4) ^ inner[None, :]).reshape(16)


def scatter_order(chip, core):
    z = chip // 4
    rows = jnp.array([[3, 2, 1, 0], [3, 2, 0, 1], [0, 1, 3, 2], [0, 1, 2, 3]])
    z_order = jnp.sum(jnp.where(jnp.arange(4)[:, None] == z, rows, 0), 0)
    inner = jnp.where(core == 0, jnp.array([3, 1, 2, 0]), jnp.array([3, 2, 1, 0]))
    return (z_order[:, None] * 4 + ((chip & 3) ^ inner)[None, :]).reshape(16)


def reduce_blocks(send, keep):
    part = []
    for k in range(4):
        rows = keep[k].shape[0] // 2
        come = permute(send[k], THIRD)
        passing = keep[k][:rows] + come[:rows]
        part.append(keep[k][rows:] + come[rows:] + permute(passing, SECOND))
    first = permute(part[0], INWARD)
    second = permute(part[1], INWARD)
    third = permute(part[2], INWARD)
    passed = permute(part[0] + first, MIDDLE)
    later = permute(part[1] + second, MIDDLE)
    last = permute(part[2] + passed, OUTWARD)
    return part[3] + third + later + last


def two_terms(x):
    upper = x.astype(jnp.bfloat16)
    return upper, (x - upper.astype(jnp.float32)).astype(jnp.bfloat16)


def dot(a, b, dims):
    return lax.dot_general(a, b, (dims, ((), ())), preferred_element_type=jnp.float32)


def dot_terms(a, b, dims=((1,), (0,))):
    return dot(a[0], b[0], dims) + (dot(a[0], b[1], dims) + dot(a[1], b[0], dims))


def beside(terms):
    return jnp.concatenate(terms, 1)


def halves(x):
    n = x.shape[1] // 2
    return x[:, :n] + x[:, n:]


def dot_rows(a, b):
    rows = jnp.concatenate([beside([b[0], b[0]]), beside([b[1], b[1]])], 0)
    return halves(dot(beside(a), rows, ((1,), (1,))))


def dot_columns(a, b):
    pair = beside(b)
    return halves(dot(beside(a), jnp.concatenate([pair, pair], 0), ((1,), (0,))))


def dot_turned(a, b):
    n = a[0].shape[1]
    out = halves(dot(beside(a), beside(b), ((0,), (0,))))
    return out[:n] + out[n:]


def three_terms(x):
    first = x.astype(jnp.bfloat16)
    rest = x - first.astype(jnp.float32)
    second = rest.astype(jnp.bfloat16)
    return first, second, (rest - second.astype(jnp.float32)).astype(jnp.bfloat16)


def dot_rows_exact(a, b):
    a, b = three_terms(a), three_terms(b)
    small = dot(beside([a[2], a[0]]), beside([b[0], b[2]]), ((1,), (1,)))
    return dot_rows(a[:2], b[:2]) + small


VMEM_LIMIT = 56 << 20


def call(kernel, name, grid, in_specs, out_specs, out_shape, scalars=0, scratch=(), aliases={}):
    return pl.pallas_call(
        kernel,
        out_shape=[jax.ShapeDtypeStruct(*shape) for shape in out_shape],
        grid_spec=pltpu.PrefetchScalarGridSpec(
            num_scalar_prefetch=scalars,
            grid=grid,
            in_specs=in_specs,
            out_specs=out_specs,
            scratch_shapes=scratch,
        ),
        input_output_aliases=aliases,
        compiler_params=pltpu.CompilerParams(vmem_limit_bytes=VMEM_LIMIT),
        name=name,
    )


def whole(x):
    return pl.BlockSpec(x.shape, lambda *_: (0,) * x.ndim)


ID_ROWS = 8


def turn_kernel(core, prompt, x, out):
    t = x[...].T
    count, rows, _ = out.shape
    half = rows - ID_ROWS
    for c in range(count):
        own = t[2 * c * half : 2 * (c + 1) * half]
        out[c, :half] = jnp.where(core[0] == 0, own[:half], own[half:])
        out[c, half:] = jnp.full((ID_ROWS, out.shape[2]), prompt[0].astype(jnp.float32))


def turn(core, prompt, hidden, chips):
    rows, model = hidden.shape
    half = model // chips // 2
    (out,) = call(
        turn_kernel,
        "turn",
        (4,),
        [pl.BlockSpec((rows, model // 4), lambda i, *_: (0, i))],
        [pl.BlockSpec((chips // 4, half + ID_ROWS, rows), lambda i, *_: (i, 0, 0))],
        [((chips, half + ID_ROWS, rows), jnp.float32)],
        scalars=2,
    )(core, prompt, hidden)
    return out


def turn_back_kernel(core, own, other, out):
    first = core[0] == 0
    parts = []
    for c in range(own.shape[0]):
        x, y = own[c], other[c]
        parts += [jnp.where(first, x, y), jnp.where(first, y, x)]
    out[...] = jnp.concatenate(parts, 0).T


def turn_back(core, back, come):
    chips, half, rows = back.shape
    steps = chips // 4
    (out,) = call(
        turn_back_kernel,
        "turn_back",
        (steps,),
        [
            pl.BlockSpec((2, half, rows), lambda i, core: (core[0] * steps + i, 0, 0)),
            pl.BlockSpec((2, half, rows), lambda i, core: (i, 0, 0)),
        ],
        [pl.BlockSpec((rows, 4 * half), lambda i, *_: (0, i))],
        [((rows, chips * half), jnp.float32)],
        scalars=1,
    )(core, back, come)
    return out


def split_kernel(core, key, value, out):
    depth, width = key.shape
    half = depth // 2
    first = core[0] == 0
    for start, ref in ((0, key), (width, value)):
        x, y = ref[:half], ref[half:]
        for row, part in ((0, jnp.where(first, x, y)), (half, jnp.where(first, y, x))):
            upper, lower = two_terms(part)
            for place, term in enumerate((upper, upper, lower)):
                top = place * depth + row
                out[top : top + half, start : start + width] = term


def split_weights(core, key, value):
    shape = ((3 * key.shape[0], 2 * key.shape[1]), jnp.bfloat16)
    (out,) = call(
        split_kernel,
        "split_weights",
        (1,),
        [whole(key), whole(value)],
        [pl.BlockSpec(shape[0], lambda *_: (0, 0))],
        [shape],
        scalars=1,
    )(core, key, value)
    return out


def project_kernel(index, *refs):
    own, other, weights, outs, x = refs[:4], refs[4:8], refs[8], refs[9:11], refs[11]

    @pl.when(pl.program_id(0) == 0)
    def _():
        both = jnp.concatenate([beside([ref[0] for ref in own]), beside([ref[0] for ref in other])], 0)
        upper, lower = two_terms(both)
        x[...] = jnp.concatenate([upper, lower, upper], 0).T

    terms = dot(x[...], weights[...], ((1,), (0,)))
    count = outs[0].shape[0]
    outs[0][...] = terms[:count]
    outs[1][...] = terms[count:]


def project(index, own, other, weights):
    _, rows, plen = own.shape
    depth, columns = weights.shape
    picked = [
        pl.BlockSpec((1, rows - ID_ROWS, plen), lambda i, index, q=q: (index[q], 0, 0))
        for q in range(4)
    ]
    return call(
        project_kernel,
        "project",
        (4,),
        picked * 2 + [pl.BlockSpec((depth, columns // 4), lambda i, *_: (0, i))],
        [pl.BlockSpec((2 * plen, columns // 4), lambda i, *_: (0, i))] * 2,
        [((2 * plen, columns), jnp.float32)] * 2,
        scalars=1,
        scratch=[pltpu.VMEM((4 * plen, depth), jnp.bfloat16)],
    )(index, *([own] * 4), *([other] * 4), weights)


def weight_times(weights, blocks):
    depth = weights.shape[0] // 3
    terms = weights[:depth], weights[2 * depth :]
    out = []
    for q in range(0, len(blocks), 2):
        x = two_terms(jnp.concatenate([blocks[q][...], blocks[q + 1][...]], 0))
        out.append(dot_terms(terms, x, ((1,), (1,))))
    return out


def hidden_part_kernel(place, *refs):
    blocks, weights, (keep, give) = refs[:-3], refs[-3], refs[-2:]
    half, plen = keep.shape[1:]
    for q, part in enumerate(weight_times(weights, blocks)):
        for i in range(2):
            piece = part[:, i * plen : (i + 1) * plen]
            keep[place[2 * q + i]] = piece[:half]
            give[place[2 * q + i]] = piece[half:]


def hidden_part(place, blocks, weights):
    shape = ((len(blocks), weights.shape[0] // 6, blocks[0].shape[0]), jnp.float32)
    return call(
        hidden_part_kernel,
        "hidden_part",
        (1,),
        [whole(x) for x in blocks] + [whole(weights)],
        [pl.BlockSpec(shape[0], lambda *_: (0, 0, 0))] * 2,
        [shape] * 2,
        scalars=1,
    )(place, *blocks, weights)


def hidden_last_kernel(place, keep_in, give_in, *refs):
    blocks, weights, (keep, give) = refs[:-3], refs[-3], refs[-2:]
    half, plen = keep.shape[1:]
    (part,) = weight_times(weights, blocks)
    for i in range(2):
        keep[place[i]] = keep_in[i]
        give[place[i]] = give_in[i]
        piece = part[:, i * plen : (i + 1) * plen]
        keep[place[2 + i]] = piece[:half]
        give[place[2 + i]] = piece[half:]


def hidden_last(place, keep, give, blocks, weights):
    shape = ((4,) + keep.shape[1:], jnp.float32)
    return call(
        hidden_last_kernel,
        "hidden_last",
        (1,),
        [whole(keep), whole(give)] + [whole(x) for x in blocks] + [whole(weights)],
        [pl.BlockSpec(shape[0], lambda *_: (0, 0, 0))] * 2,
        [shape] * 2,
        scalars=1,
    )(place, keep, give, *blocks, weights)


def assemble_kernel(listed, *refs):
    keep, come, out = refs[:4], refs[4:8], refs[8]
    for k in range(4):
        for i in range(4):
            out[listed[4 * k + i]] = keep[k][i] + come[k][i]


def assemble(listed, keep, come):
    shape = ((16,) + keep[0].shape[1:], jnp.float32)
    (out,) = call(
        assemble_kernel,
        "assemble",
        (1,),
        [whole(x) for x in keep + come],
        [pl.BlockSpec(shape[0], lambda *_: (0, 0, 0))],
        [shape],
        scalars=1,
    )(listed, *keep, *come)
    return out


def weight_grad_kernel(listed, core, own, other, *refs):
    blocks, outs = refs[:-2], refs[-2:]
    half = own.shape[1] - ID_ROWS
    width = outs[0].shape[1]
    total = None
    for q in range(0, len(blocks), 4):
        x = jnp.concatenate(
            [beside([ref[listed[q + i], :half] for i in range(4)]) for ref in (own, other)], 0
        )
        g = jnp.concatenate([ref[...] for ref in blocks[q : q + 4]], 0)
        term = dot_terms(two_terms(x), two_terms(g))
        total = term if total is None else total + term
    x, y = total[:half], total[half:]
    first = core[0] == 0
    for row, part in ((0, jnp.where(first, x, y)), (half, jnp.where(first, y, x))):
        for out, start in zip(outs, (0, width)):
            out[row : row + half] = part[:, start : start + width]


def weight_grad(listed, core, own, other, blocks):
    plen, columns = blocks[0].shape
    shape = ((2 * (own.shape[1] - ID_ROWS), columns // 2), jnp.float32)
    return call(
        weight_grad_kernel,
        "weight_grad",
        (1,),
        [whole(own)] * 2 + [whole(blocks[0])] * len(blocks),
        [pl.BlockSpec(shape[0], lambda *_: (0, 0))] * 2,
        [shape] * 2,
        scalars=2,
    )(listed, core, own, other, *blocks)


SCALE = 1.0 / math.sqrt(HEAD_SIZE)
PER_GROUP = QUERY_HEADS // KEY_VALUE_HEADS


def stack(ref):
    size = ref.shape[1] // PER_GROUP
    return jnp.concatenate([ref[:, h * size : (h + 1) * size] for h in range(PER_GROUP)], 0)


def unstack(ref, x):
    rows, size = ref.shape[0], ref.shape[1] // PER_GROUP
    for h in range(PER_GROUP):
        ref[:, h * size : (h + 1) * size] = x[h * rows : (h + 1) * rows]


def save_columns(ref, first, second):
    rows = ref.shape[0]
    lane = lax.broadcasted_iota(jnp.int32, ref.shape, 1)
    out = jnp.zeros(ref.shape, jnp.float32)
    for start, column in ((0, first), (8, second)):
        for h in range(PER_GROUP):
            out = jnp.where(lane == start + h, column[h * rows : (h + 1) * rows], out)
    ref[...] = out


def load_column(ref, start):
    return jnp.concatenate([ref[:, start + h : start + h + 1] for h in range(PER_GROUP)], 0)


def row_number(shape, rows):
    return lax.broadcasted_iota(jnp.int32, shape, 0) % rows


def own_scores(length, query, keys, rows):
    scores = dot_rows_exact(query, keys) * SCALE
    j = lax.broadcasted_iota(jnp.int32, scores.shape, 1)
    return jnp.where((j <= row_number(scores.shape, rows)) & (j < length), scores, masked_value)


def open_kernel(length, q, k, v, total, stats):
    scores = own_scores(length[0], stack(q), k[...], q.shape[0])
    top = jnp.max(scores, -1, keepdims=True)
    expo = jnp.exp(scores - top)
    unstack(total, dot_columns(two_terms(expo), two_terms(v[...])))
    save_columns(stats, top, jnp.sum(expo, -1, keepdims=True))


def close_kernel(length, q, g, kp, vp, total, stats, out, grad_scores, stats_out, gk, gv):
    query, keys, values = stack(q), kp[...], vp[...]
    scores = dot_rows_exact(query, keys) * SCALE
    before = load_column(stats, 0)
    top = jnp.maximum(before, jnp.max(scores, -1, keepdims=True))
    weight = jnp.exp(before - top)
    expo = jnp.exp(scores - top)
    denominator = weight * load_column(stats, 8) + jnp.sum(expo, -1, keepdims=True)
    inverse = 1.0 / denominator
    prob = expo * inverse
    prob_terms, value_terms = two_terms(prob), two_terms(values)
    result = (weight * inverse) * stack(total) + dot_columns(prob_terms, value_terms)
    valid = row_number(result.shape, q.shape[0]) < length[0]
    result = jnp.where(valid, result, 0.0)
    upstream = jnp.where(valid, stack(g), 0.0)
    upstream_terms = two_terms(upstream)
    inner = jnp.sum(upstream * result, -1, keepdims=True)
    grad = prob * (dot_rows(upstream_terms, value_terms) - inner) * SCALE
    unstack(out, result)
    unstack(grad_scores, grad)
    save_columns(stats_out, top + jnp.log(denominator), inner)
    gk[...] = dot_turned(two_terms(grad), two_terms(query))
    gv[...] = dot_turned(prob_terms, upstream_terms)


def finish_kernel(length, q, g, k, v, kp, grad_scores, stats, gq, gk, gv):
    query, keys = stack(q), k[...]
    rows = q.shape[0]
    prob = jnp.exp(own_scores(length[0], query, keys, rows) - load_column(stats, 0))
    upstream = stack(g)
    upstream = jnp.where(row_number(upstream.shape, rows) < length[0], upstream, 0.0)
    upstream_terms = two_terms(upstream)
    grad = prob * (dot_rows(upstream_terms, two_terms(v[...])) - load_column(stats, 8)) * SCALE
    grad_terms = two_terms(grad)
    prompt_part = dot_columns(two_terms(stack(grad_scores)), two_terms(kp[...]))
    unstack(gq, prompt_part + dot_columns(grad_terms, two_terms(keys)))
    gk[...] = dot_turned(grad_terms, two_terms(query))
    gv[...] = dot_turned(two_terms(prob), upstream_terms)


def attention(kernel, name, groups, length, ins, outs, start=0, count=None, into=()):
    def body(length, *refs):
        kernel(length, *refs[: len(ins)], *refs[len(ins) + len(into) :])

    return call(
        body,
        name,
        (groups if count is None else count,),
        [
            pl.BlockSpec((x.shape[0], size), lambda i, *_, skip=skip: (0, skip + start + i))
            for x, size, skip in ins
        ]
        + [pl.BlockSpec(memory_space=pl.ANY)] * len(into),
        [pl.BlockSpec(shape, lambda i, *_: (0, start + i)) for shape in outs],
        [((rows, groups * size), jnp.float32) for rows, size in outs],
        scalars=1,
        aliases={1 + len(ins) + i: i for i in range(len(into))},
    )(length, *(x for x, _, _ in ins), *into)


def take_blocks(x, index):
    return jnp.stack(
        [lax.dynamic_index_in_dim(x, index[j], keepdims=False) for j in range(index.shape[0])]
    )


def take_small(table, index):
    hit = index[..., None] == jnp.arange(table.shape[0])
    return jnp.sum(jnp.where(hit, table, 0), -1)


def per_device(
    short,
    prompt_hidden,
    key_weight,
    value_weight,
    queries,
    keys_resp,
    response_value_rows,
    grad_out,
    resp_prompt,
    resp_len,
):
    chips = lax.axis_size("dp")
    chip, core = lax.axis_index("dp"), lax.axis_index("mp")
    rows_own, model = prompt_hidden.shape
    slice_width = model // chips
    width = key_weight.shape[1]
    groups = width // HEAD_SIZE
    plen = rows_own * chips // PROMPT_COUNT
    tokens = queries.shape[0]
    responses = tokens * chips // RESPONSE_LENGTH
    assert tokens == RESPONSE_LENGTH
    short = short and responses == PROMPT_COUNT
    here = core.astype(jnp.int32)[None]
    wide = PER_GROUP * HEAD_SIZE

    if short:
        mine = lax.all_to_all(turn(here, resp_prompt, prompt_hidden, chips), "dp", 0, 0)
        weight_terms = split_weights(here, key_weight, value_weight)
    else:
        all_prompts = lax.all_gather(resp_prompt, "dp", axis=0, tiled=True)
        hidden = lax.all_to_all(
            prompt_hidden.reshape(rows_own, chips, slice_width).transpose(1, 0, 2), "dp", 0, 0
        )
        hidden = hidden.reshape(PROMPT_COUNT, plen, slice_width)
        weights = jnp.concatenate([key_weight, value_weight], 1)

    q = (queries, wide, 0)
    total, stats = attention(
        open_kernel,
        "open",
        groups,
        resp_len,
        [q, (keys_resp, HEAD_SIZE, 0), (response_value_rows, HEAD_SIZE, 0)],
        [(tokens, wide), (tokens, HEAD_SIZE)],
    )

    if short:
        mine, weight_terms, total, stats = lax.optimization_barrier(
            (mine, weight_terms, total, stats)
        )
        all_prompts = mine[:, slice_width // 2, 0].astype(jnp.int32)
        other = lax.ppermute(mine, "mp", SWAP)
        listed = take_small(all_prompts, scatter_order(chip, core))
        pairs = [project(listed[4 * k : 4 * k + 4], mine, other, weight_terms) for k in range(4)]
        prompt_rows = reduce_blocks([pair[0] for pair in pairs], [pair[1] for pair in pairs])
    else:
        terms = jnp.einsum("rtc,ck->rtk", take_blocks(hidden, all_prompts), weights, precision=HIGH)
        prompt_rows = lax.psum_scatter(
            terms.reshape(responses * plen, 2 * width), "dp", scatter_dimension=0, tiled=True
        )

    g = (grad_out, wide, 0)
    prompt_keys = (prompt_rows, HEAD_SIZE, 0)
    result, grad_scores, stats, own_k, own_v = attention(
        close_kernel,
        "close",
        groups,
        resp_len,
        [q, g, prompt_keys, (prompt_rows, HEAD_SIZE, groups), (total, wide, 0), (stats, HEAD_SIZE, 0)],
        [(tokens, wide), (tokens, PER_GROUP * plen), (tokens, HEAD_SIZE)] + [(plen, HEAD_SIZE)] * 2,
    )
    finish_ins = [q, g, (keys_resp, HEAD_SIZE, 0), (response_value_rows, HEAD_SIZE, 0), prompt_keys]
    finish_ins += [(grad_scores, PER_GROUP * plen, 0), (stats, HEAD_SIZE, 0)]
    finish_outs = [(tokens, wide)] + [(tokens, HEAD_SIZE)] * 2
    finish = functools.partial(
        attention, finish_kernel, "finish", groups, resp_len, finish_ins, finish_outs
    )

    own = jnp.concatenate([own_k, own_v], 1)
    if short:
        place = gathered_order(chip, core)[:4] ^ chip
        listed = take_small(all_prompts, chip ^ jnp.arange(chips))
        far = [own] + [permute(own, ACROSS[k]) for k in range(1, 4)]
        near, third, both = [permute(own, SECOND)], [permute(own, THIRD)], []
        keep, give, state = [], [], ()

        def group(k):
            return [far[k], near[k], third[k], both[k]]

        for k in range(1, 4):
            done = hidden_part(place, group(0), weight_terms) if k == 3 else None
            state = finish(start=k - 1, count=1, into=state) if k < 3 else state
            far[k], near[k - 1], state, done = lax.optimization_barrier(
                (far[k], near[k - 1], state, done)
            )
            both.append(permute(near[k - 1], THIRD))
            near.append(permute(far[k], SECOND))
            third.append(permute(far[k], THIRD))
        parts = [done]
        near[3], done = lax.optimization_barrier(
            (near[3], hidden_part(place, group(1), weight_terms))
        )
        both.append(permute(near[3], THIRD))
        parts.append(done)
        parts.append(hidden_part(place, group(2), weight_terms))
        come = [lax.ppermute(give, "mp", SWAP) for _, give in parts]
        pair = hidden_part(jnp.arange(2), [far[3], near[3]], weight_terms)
        third[3], both[3], parts, come, pair = lax.optimization_barrier(
            (third[3], both[3], parts, come, pair)
        )
        parts.append(hidden_last(place, *pair, [third[3], both[3]], weight_terms))
        come.append(lax.ppermute(parts[3][1], "mp", SWAP))
        back = lax.all_to_all(assemble(listed, [x for x, _ in parts], come), "dp", 0, 0)

        order = take_small(all_prompts, gathered_order(chip, core))
        gathered = [x for k in range(4) for x in group(k)]
        grad_w_key, grad_w_value = weight_grad(order, here, mine, other, gathered)
        state = finish(start=2, count=groups - 2, into=state)
        back, grad_w_key, grad_w_value, state = lax.optimization_barrier(
            (back, grad_w_key, grad_w_value, state)
        )
        grad_query, grad_keys, grad_values = state
        leave = jnp.where(core == 0, back[chips // 2 :], back[: chips // 2])
        grad_hidden = turn_back(here, back, lax.ppermute(leave, "mp", SWAP))
    else:
        grad_query, grad_keys, grad_values = finish()
        gathered = lax.all_gather(own, "dp", axis=0, tiled=True).reshape(responses, plen, 2 * width)
        summed = jnp.einsum(
            "rtc,rtk->ck", take_blocks(hidden, all_prompts), gathered, precision=HIGH
        )
        grad_w_key, grad_w_value = summed[:, :width], summed[:, width:]
        terms = jnp.einsum("rtk,ck->rtc", gathered, weights, precision=HIGH)
        numbers = jnp.arange(responses)
        same = all_prompts[:, None] == all_prompts[None, :]
        earlier = jnp.sum(same & (numbers[None, :] < numbers[:, None]), 1)
        hidden_terms = 0.0
        for i in range(responses // PROMPT_COUNT):
            hit = (all_prompts[None, :] == jnp.arange(PROMPT_COUNT)[:, None]) & (earlier[None, :] == i)
            place = jnp.sum(jnp.where(hit, numbers[None, :], 0), -1)
            hidden_terms = hidden_terms + take_blocks(terms, place)
        back = lax.all_to_all(hidden_terms.reshape(chips, rows_own, slice_width), "dp", 0, 0)
        back = back.transpose(1, 0, 2).reshape(rows_own, model)
        grad_hidden = lax.psum_scatter(back, "mp", scatter_dimension=1, tiled=True)
    return (
        result,
        grad_query,
        grad_keys,
        grad_values,
        grad_hidden,
        grad_w_key,
        grad_w_value,
    )


def solution(mesh):
    short = mesh.shape["dp"] == 16 and mesh.shape["mp"] == 2
    in_specs = (P("dp", None),) + (P("dp", "mp"),) * 6 + (P("dp"),) * 2
    out_specs = (P("dp", "mp"),) * 7
    return jax.shard_map(
        functools.partial(per_device, short),
        mesh=mesh,
        in_specs=in_specs,
        out_specs=out_specs,
        check_vma=False,
    )
```

```python
import functools
import math

import jax
import jax.numpy as jnp
from jax import lax
from jax.experimental import pallas as pl
from jax.experimental.pallas import tpu as pltpu
from jax.sharding import PartitionSpec as P

QUERY_HEADS = 40
KEY_VALUE_HEADS = 8
HEAD_SIZE = 128
PROMPT_COUNT = 16
RESPONSE_LENGTH = 256

masked_value = -1e30
HIGH = lax.Precision.HIGH
BOTH = ("dp", "mp")


def pairs_of(target):
    return [
        (c * 2 + m, target(c, m) * 2 + m)
        for c in range(16)
        for m in range(2)
        if target(c, m) is not None
    ]


def along_z(moves):
    return pairs_of(lambda c, m: moves[c >> 2] << 2 | c & 3 if c >> 2 in moves else None)


SECOND = pairs_of(lambda c, m: c ^ (2, 1)[m])
THIRD = pairs_of(lambda c, m: c ^ (1, 2)[m])
ACROSS = [along_z({z: z ^ k for z in range(4)}) for k in range(4)]
MIDDLE = along_z({1: 2, 2: 1})
INWARD = along_z({0: 1, 3: 2})
OUTWARD = along_z({1: 0, 2: 3})
SWAP = [(0, 1), (1, 0)]


def permute(x, pairs):
    return lax.ppermute(x, BOTH, pairs)


def gathered_order(chip, core):
    inner = jnp.where(core == 0, jnp.array([0, 2, 1, 3]), jnp.array([0, 1, 2, 3]))
    return (chip ^ (jnp.arange(4)[:, None] * 4) ^ inner[None, :]).reshape(16)


def scatter_order(chip, core):
    z = chip // 4
    rows = jnp.array([[3, 2, 1, 0], [3, 2, 0, 1], [0, 1, 3, 2], [0, 1, 2, 3]])
    z_order = jnp.sum(jnp.where(jnp.arange(4)[:, None] == z, rows, 0), 0)
    inner = jnp.where(core == 0, jnp.array([3, 1, 2, 0]), jnp.array([3, 2, 1, 0]))
    return (z_order[:, None] * 4 + ((chip & 3) ^ inner)[None, :]).reshape(16)


def reduce_blocks(send, keep):
    part = []
    for k in range(4):
        rows = keep[k].shape[0] // 2
        come = permute(send[k], THIRD)
        passing = keep[k][:rows] + come[:rows]
        part.append(keep[k][rows:] + come[rows:] + permute(passing, SECOND))
    first = permute(part[0], INWARD)
    second = permute(part[1], INWARD)
    third = permute(part[2], INWARD)
    passed = permute(part[0] + first, MIDDLE)
    later = permute(part[1] + second, MIDDLE)
    last = permute(part[2] + passed, OUTWARD)
    return part[3] + third + later + last


def two_terms(x):
    upper = x.astype(jnp.bfloat16)
    return upper, (x - upper.astype(jnp.float32)).astype(jnp.bfloat16)


def dot(a, b, dims):
    return lax.dot_general(a, b, (dims, ((), ())), preferred_element_type=jnp.float32)


def dot_terms(a, b, dims=((1,), (0,))):
    return dot(a[0], b[0], dims) + (dot(a[0], b[1], dims) + dot(a[1], b[0], dims))


def beside(terms):
    return jnp.concatenate(terms, 1)


def halves(x):
    n = x.shape[1] // 2
    return x[:, :n] + x[:, n:]


def dot_rows(a, b):
    rows = jnp.concatenate([beside([b[0], b[0]]), beside([b[1], b[1]])], 0)
    return halves(dot(beside(a), rows, ((1,), (1,))))


def dot_columns(a, b):
    pair = beside(b)
    return halves(dot(beside(a), jnp.concatenate([pair, pair], 0), ((1,), (0,))))


def dot_turned(a, b):
    n = a[0].shape[1]
    out = halves(dot(beside(a), beside(b), ((0,), (0,))))
    return out[:n] + out[n:]


def three_terms(x):
    first = x.astype(jnp.bfloat16)
    rest = x - first.astype(jnp.float32)
    second = rest.astype(jnp.bfloat16)
    return first, second, (rest - second.astype(jnp.float32)).astype(jnp.bfloat16)


def dot_rows_exact(a, b):
    b = three_terms(b)
    small = dot(beside([a[2], a[0]]), beside([b[0], b[2]]), ((1,), (1,)))
    return dot_rows(a[:2], b[:2]) + small


VMEM_LIMIT = 40 << 20
WHOLE_LIMIT = 32 << 20


def call(kernel, name, grid, in_specs, out_specs, out_shape, scalars=0, limit=VMEM_LIMIT):
    return pl.pallas_call(
        kernel,
        out_shape=[jax.ShapeDtypeStruct(*shape) for shape in out_shape],
        grid_spec=pltpu.PrefetchScalarGridSpec(
            num_scalar_prefetch=scalars, grid=grid, in_specs=in_specs, out_specs=out_specs
        ),
        compiler_params=pltpu.CompilerParams(vmem_limit_bytes=limit),
        name=name,
    )


def call_whole(kernel, name, ins, out_shape, scalars=0):
    vmem = pl.BlockSpec(memory_space=pltpu.VMEM)
    return pl.pallas_call(
        kernel,
        out_shape=[jax.ShapeDtypeStruct(*shape) for shape in out_shape],
        in_specs=[pl.BlockSpec(memory_space=pltpu.SMEM)] * scalars + [vmem] * (len(ins) - scalars),
        out_specs=[vmem] * len(out_shape),
        compiler_params=pltpu.CompilerParams(vmem_limit_bytes=WHOLE_LIMIT),
        name=name,
    )(*ins)


ID_ROWS = 8


def turn_kernel(core, prompt, x, out):
    t = x[...].T
    count, rows, _ = out.shape
    half = rows - ID_ROWS
    for c in range(count):
        own = t[2 * c * half : 2 * (c + 1) * half]
        out[c, :half] = jnp.where(core[0] == 0, own[:half], own[half:])
        out[c, half:] = jnp.full((ID_ROWS, out.shape[2]), prompt[0].astype(jnp.float32))


def turn(core, prompt, hidden, chips):
    rows, model = hidden.shape
    half = model // chips // 2
    (out,) = call(
        turn_kernel,
        "turn",
        (4,),
        [pl.BlockSpec((rows, model // 4), lambda i, *_: (0, i))],
        [pl.BlockSpec((chips // 4, half + ID_ROWS, rows), lambda i, *_: (i, 0, 0))],
        [((chips, half + ID_ROWS, rows), jnp.float32)],
        scalars=2,
    )(core, prompt, hidden)
    return out


def turn_back_kernel(core, own, other, out):
    first = core[0] == 0
    parts = []
    for c in range(own.shape[0]):
        x, y = own[c], other[c]
        parts += [jnp.where(first, x, y), jnp.where(first, y, x)]
    out[...] = jnp.concatenate(parts, 0).T


def turn_back(core, back, come):
    chips, half, rows = back.shape
    steps = chips // 4
    (out,) = call(
        turn_back_kernel,
        "turn_back",
        (steps,),
        [
            pl.BlockSpec((2, half, rows), lambda i, core: (core[0] * steps + i, 0, 0)),
            pl.BlockSpec((2, half, rows), lambda i, core: (i, 0, 0)),
        ],
        [pl.BlockSpec((rows, 4 * half), lambda i, *_: (0, i))],
        [((rows, chips * half), jnp.float32)],
        scalars=1,
    )(core, back, come)
    return out


def split_kernel(core, key, value, out):
    depth, width = key.shape
    half = depth // 2
    first = core[0] == 0
    for start, ref in ((0, key), (width, value)):
        x, y = ref[:half], ref[half:]
        for row, part in ((0, jnp.where(first, x, y)), (half, jnp.where(first, y, x))):
            upper, lower = two_terms(part)
            for place, term in enumerate((upper, upper, lower)):
                top = place * depth + row
                out[top : top + half, start : start + width] = term


def split_weights(core, key, value):
    shape = (3 * key.shape[0], 2 * key.shape[1])
    (out,) = call_whole(
        split_kernel, "split_weights", [core, key, value], [(shape, jnp.bfloat16)], scalars=1
    )
    return out


def project_kernel(index, own, other, weights, send, keep):
    half = own.shape[1] - ID_ROWS
    both = jnp.concatenate(
        [beside([ref[index[q], :half] for q in range(4)]) for ref in (own, other)], 0
    )
    upper, lower = two_terms(both)
    terms = dot(jnp.concatenate([upper, lower, upper], 0).T, weights[...], ((1,), (0,)))
    count = send.shape[0]
    send[...] = terms[:count]
    keep[...] = terms[count:]


def project(index, own, other, weights):
    shape = ((2 * own.shape[2], weights.shape[1]), jnp.float32)
    return call_whole(
        project_kernel, "project", [index, own, other, weights], [shape] * 2, scalars=1
    )


def weight_times(weights, blocks):
    depth = weights.shape[0] // 3
    terms = weights[:depth], weights[2 * depth :]
    out = []
    for q in range(0, len(blocks), 2):
        x = two_terms(jnp.concatenate([blocks[q][...], blocks[q + 1][...]], 0))
        out.append(dot_terms(terms, x, ((1,), (1,))))
    return out


def hidden_part_kernel(place, *refs):
    blocks, weights, (keep, give) = refs[:-3], refs[-3], refs[-2:]
    half, plen = keep.shape[1:]
    for q, part in enumerate(weight_times(weights, blocks)):
        for i in range(2):
            piece = part[:, i * plen : (i + 1) * plen]
            keep[place[2 * q + i]] = piece[:half]
            give[place[2 * q + i]] = piece[half:]


def hidden_part(place, blocks, weights):
    shape = ((len(blocks), weights.shape[0] // 6, blocks[0].shape[0]), jnp.float32)
    return call_whole(
        hidden_part_kernel, "hidden_part", [place, *blocks, weights], [shape] * 2, scalars=1
    )


def hidden_last_kernel(place, keep_in, give_in, *refs):
    blocks, weights, (keep, give) = refs[:-3], refs[-3], refs[-2:]
    half, plen = keep.shape[1:]
    (part,) = weight_times(weights, blocks)
    for i in range(2):
        keep[place[i]] = keep_in[i]
        give[place[i]] = give_in[i]
        piece = part[:, i * plen : (i + 1) * plen]
        keep[place[2 + i]] = piece[:half]
        give[place[2 + i]] = piece[half:]


def hidden_last(place, keep, give, blocks, weights):
    shape = ((4,) + keep.shape[1:], jnp.float32)
    return call_whole(
        hidden_last_kernel,
        "hidden_last",
        [place, keep, give, *blocks, weights],
        [shape] * 2,
        scalars=1,
    )


def assemble_kernel(listed, *refs):
    keep, come, out = refs[:4], refs[4:8], refs[8]
    for k in range(4):
        for i in range(4):
            out[listed[4 * k + i]] = keep[k][i] + come[k][i]


def assemble(listed, keep, come):
    shape = ((16,) + keep[0].shape[1:], jnp.float32)
    (out,) = call_whole(assemble_kernel, "assemble", [listed, *keep, *come], [shape], scalars=1)
    return out


def weight_grad_kernel(listed, core, own, other, *refs):
    blocks, outs = refs[:-2], refs[-2:]
    half = own.shape[1] - ID_ROWS
    width = outs[0].shape[1]
    total = None
    for q in range(0, len(blocks), 4):
        x = jnp.concatenate(
            [beside([ref[listed[q + i], :half] for i in range(4)]) for ref in (own, other)], 0
        )
        g = jnp.concatenate([ref[...] for ref in blocks[q : q + 4]], 0)
        term = dot_terms(two_terms(x), two_terms(g))
        total = term if total is None else total + term
    x, y = total[:half], total[half:]
    first = core[0] == 0
    for row, part in ((0, jnp.where(first, x, y)), (half, jnp.where(first, y, x))):
        for out, start in zip(outs, (0, width)):
            out[row : row + half] = part[:, start : start + width]


def weight_grad(listed, core, own, other, blocks):
    plen, columns = blocks[0].shape
    shape = ((2 * (own.shape[1] - ID_ROWS), columns // 2), jnp.float32)
    return call_whole(
        weight_grad_kernel,
        "weight_grad",
        [listed, core, own, other, *blocks],
        [shape] * 2,
        scalars=2,
    )


SCALE = 1.0 / math.sqrt(HEAD_SIZE)
PER_GROUP = QUERY_HEADS // KEY_VALUE_HEADS


def stack(ref):
    size = ref.shape[1] // PER_GROUP
    return jnp.concatenate([ref[:, h * size : (h + 1) * size] for h in range(PER_GROUP)], 0)


def unstack(ref, x):
    rows, size = ref.shape[0], ref.shape[1] // PER_GROUP
    for h in range(PER_GROUP):
        ref[:, h * size : (h + 1) * size] = x[h * rows : (h + 1) * rows]


def save_columns(ref, first, second):
    rows = ref.shape[0]
    lane = lax.broadcasted_iota(jnp.int32, ref.shape, 1)
    out = jnp.zeros(ref.shape, jnp.float32)
    for start, column in ((0, first), (8, second)):
        for h in range(PER_GROUP):
            out = jnp.where(lane == start + h, column[h * rows : (h + 1) * rows], out)
    ref[...] = out


def load_column(ref, start):
    return jnp.concatenate([ref[:, start + h : start + h + 1] for h in range(PER_GROUP)], 0)


def row_number(shape, rows):
    return lax.broadcasted_iota(jnp.int32, shape, 0) % rows


def own_scores(length, query, keys, rows):
    scores = dot_rows_exact(query, keys) * SCALE
    j = lax.broadcasted_iota(jnp.int32, scores.shape, 1)
    return jnp.where((j <= row_number(scores.shape, rows)) & (j < length), scores, masked_value)


def open_kernel(length, q, g, k, v, total, stats, q1, q2, q3, g1, g2):
    query_terms = three_terms(stack(q))
    for ref, term in zip((q1, q2, q3), query_terms):
        unstack(ref, term)
    upstream = stack(g)
    upstream = jnp.where(row_number(upstream.shape, q.shape[0]) < length[0], upstream, 0.0)
    for ref, term in zip((g1, g2), two_terms(upstream)):
        unstack(ref, term)
    scores = own_scores(length[0], query_terms, k[...], q.shape[0])
    top = jnp.max(scores, -1, keepdims=True)
    expo = jnp.exp(scores - top)
    unstack(total, dot_columns(two_terms(expo), two_terms(v[...])))
    save_columns(stats, top, jnp.sum(expo, -1, keepdims=True))


def close_kernel(length, q1, q2, q3, g, g1, g2, kp, vp, total, stats, out, grad_scores, stats_out, gk, gv):
    query_terms = stack(q1), stack(q2), stack(q3)
    scores = dot_rows_exact(query_terms, kp[...]) * SCALE
    before = load_column(stats, 0)
    top = jnp.maximum(before, jnp.max(scores, -1, keepdims=True))
    weight = jnp.exp(before - top)
    expo = jnp.exp(scores - top)
    denominator = weight * load_column(stats, 8) + jnp.sum(expo, -1, keepdims=True)
    inverse = 1.0 / denominator
    prob = expo * inverse
    prob_terms, value_terms = two_terms(prob), two_terms(vp[...])
    result = (weight * inverse) * stack(total) + dot_columns(prob_terms, value_terms)
    result = jnp.where(row_number(result.shape, g.shape[0]) < length[0], result, 0.0)
    upstream_terms = stack(g1), stack(g2)
    inner = jnp.sum(stack(g) * result, -1, keepdims=True)
    grad = prob * (dot_rows(upstream_terms, value_terms) - inner) * SCALE
    unstack(out, result)
    unstack(grad_scores, grad)
    save_columns(stats_out, top + jnp.log(denominator), inner)
    gk[...] = dot_turned(two_terms(grad), query_terms[:2])
    gv[...] = dot_turned(prob_terms, upstream_terms)


def finish_kernel(length, q1, q2, q3, g1, g2, k, v, kp, grad_scores, stats, gq, gk, gv):
    query_terms, keys = (stack(q1), stack(q2), stack(q3)), k[...]
    prob = jnp.exp(own_scores(length[0], query_terms, keys, q1.shape[0]) - load_column(stats, 0))
    upstream_terms = stack(g1), stack(g2)
    grad = prob * (dot_rows(upstream_terms, two_terms(v[...])) - load_column(stats, 8)) * SCALE
    grad_terms = two_terms(grad)
    prompt_part = dot_columns(two_terms(stack(grad_scores)), two_terms(kp[...]))
    unstack(gq, prompt_part + dot_columns(grad_terms, two_terms(keys)))
    gk[...] = dot_turned(grad_terms, query_terms[:2])
    gv[...] = dot_turned(two_terms(prob), upstream_terms)


def attention(kernel, name, groups, length, ins, outs):
    return call(
        kernel,
        name,
        (groups,),
        [
            pl.BlockSpec((x.shape[0], size), lambda i, *_, skip=skip: (0, skip + i))
            for x, size, skip in ins
        ],
        [pl.BlockSpec((rows, size), lambda i, *_: (0, i)) for rows, size, _ in outs],
        [((rows, groups * size), kind) for rows, size, kind in outs],
        scalars=1,
    )(length, *(x for x, _, _ in ins))


def take_blocks(x, index):
    return jnp.stack(
        [lax.dynamic_index_in_dim(x, index[j], keepdims=False) for j in range(index.shape[0])]
    )


def take_small(table, index):
    hit = index[..., None] == jnp.arange(table.shape[0])
    return jnp.sum(jnp.where(hit, table, 0), -1)


def per_device(
    short,
    prompt_hidden,
    key_weight,
    value_weight,
    queries,
    keys_resp,
    response_value_rows,
    grad_out,
    resp_prompt,
    resp_len,
):
    chips = lax.axis_size("dp")
    chip, core = lax.axis_index("dp"), lax.axis_index("mp")
    rows_own, model = prompt_hidden.shape
    slice_width = model // chips
    width = key_weight.shape[1]
    groups = width // HEAD_SIZE
    plen = rows_own * chips // PROMPT_COUNT
    tokens = queries.shape[0]
    responses = tokens * chips // RESPONSE_LENGTH
    assert tokens == RESPONSE_LENGTH
    short = short and responses == PROMPT_COUNT
    here = core.astype(jnp.int32)[None]
    wide = PER_GROUP * HEAD_SIZE

    if short:
        mine = lax.all_to_all(turn(here, resp_prompt, prompt_hidden, chips), "dp", 0, 0)
        weight_terms = split_weights(here, key_weight, value_weight)
    else:
        all_prompts = lax.all_gather(resp_prompt, "dp", axis=0, tiled=True)
        hidden = lax.all_to_all(
            prompt_hidden.reshape(rows_own, chips, slice_width).transpose(1, 0, 2), "dp", 0, 0
        )
        hidden = hidden.reshape(PROMPT_COUNT, plen, slice_width)
        weights = jnp.concatenate([key_weight, value_weight], 1)

    whole_heads, one_head = (tokens, wide, jnp.float32), (tokens, HEAD_SIZE, jnp.float32)
    total, stats, *kept = attention(
        open_kernel,
        "open",
        groups,
        resp_len,
        [
            (queries, wide, 0),
            (grad_out, wide, 0),
            (keys_resp, HEAD_SIZE, 0),
            (response_value_rows, HEAD_SIZE, 0),
        ],
        [whole_heads, one_head] + [(tokens, wide, jnp.bfloat16)] * 5,
    )

    if short:
        mine, weight_terms, total, stats, kept = lax.optimization_barrier(
            (mine, weight_terms, total, stats, kept)
        )
        all_prompts = mine[:, slice_width // 2, 0].astype(jnp.int32)
        other = lax.ppermute(mine, "mp", SWAP)
        listed = take_small(all_prompts, scatter_order(chip, core))
        pairs = [project(listed[4 * k : 4 * k + 4], mine, other, weight_terms) for k in range(4)]
        prompt_rows = reduce_blocks([pair[0] for pair in pairs], [pair[1] for pair in pairs])
    else:
        terms = jnp.einsum("rtc,ck->rtk", take_blocks(hidden, all_prompts), weights, precision=HIGH)
        prompt_rows = lax.psum_scatter(
            terms.reshape(responses * plen, 2 * width), "dp", scatter_dimension=0, tiled=True
        )

    query_terms = [(x, wide, 0) for x in kept[:3]]
    upstream_terms = [(x, wide, 0) for x in kept[3:]]
    prompt_keys = (prompt_rows, HEAD_SIZE, 0)
    result, grad_scores, stats, own_k, own_v = attention(
        close_kernel,
        "close",
        groups,
        resp_len,
        query_terms
        + [(grad_out, wide, 0)]
        + upstream_terms
        + [prompt_keys, (prompt_rows, HEAD_SIZE, groups), (total, wide, 0), (stats, HEAD_SIZE, 0)],
        [whole_heads, (tokens, PER_GROUP * plen, jnp.float32), one_head]
        + [(plen, HEAD_SIZE, jnp.float32)] * 2,
    )

    def finish(stats):
        own_ins = [(keys_resp, HEAD_SIZE, 0), (response_value_rows, HEAD_SIZE, 0), prompt_keys]
        kept_ins = [(grad_scores, PER_GROUP * plen, 0), (stats, HEAD_SIZE, 0)]
        return attention(
            finish_kernel,
            "finish",
            groups,
            resp_len,
            query_terms + upstream_terms + own_ins + kept_ins,
            [whole_heads] + [one_head] * 2,
        )

    own = jnp.concatenate([own_k, own_v], 1)
    if short:
        place = gathered_order(chip, core)[:4] ^ chip
        listed = take_small(all_prompts, chip ^ jnp.arange(chips))
        far = [own] + [permute(own, ACROSS[k]) for k in range(1, 4)]
        near, third, both = [permute(own, SECOND)], [permute(own, THIRD)], []

        def group(k):
            return [far[k], near[k], third[k], both[k]]

        for k in range(1, 4):
            done = hidden_part(place, group(0), weight_terms) if k == 3 else None
            far[k], near[k - 1], done = lax.optimization_barrier((far[k], near[k - 1], done))
            both.append(permute(near[k - 1], THIRD))
            near.append(permute(far[k], SECOND))
            third.append(permute(far[k], THIRD))
        parts = [done]
        near[3], done = lax.optimization_barrier(
            (near[3], hidden_part(place, group(1), weight_terms))
        )
        both.append(permute(near[3], THIRD))
        parts.append(done)
        parts.append(hidden_part(place, group(2), weight_terms))
        come = [lax.ppermute(give, "mp", SWAP) for _, give in parts]
        pair = hidden_part(jnp.arange(2), [far[3], near[3]], weight_terms)
        third[3], both[3], parts, come, pair, stats_late = lax.optimization_barrier(
            (third[3], both[3], parts, come, pair, stats)
        )
        parts.append(hidden_last(place, *pair, [third[3], both[3]], weight_terms))
        come.append(lax.ppermute(parts[3][1], "mp", SWAP))
        back = lax.all_to_all(assemble(listed, [x for x, _ in parts], come), "dp", 0, 0)

        order = take_small(all_prompts, gathered_order(chip, core))
        gathered = [x for k in range(4) for x in group(k)]
        grad_w_key, grad_w_value = weight_grad(order, here, mine, other, gathered)
        back, grad_w_key, grad_w_value, state = lax.optimization_barrier(
            (back, grad_w_key, grad_w_value, finish(stats_late))
        )
        grad_query, grad_keys, grad_values = state
        leave = jnp.where(core == 0, back[chips // 2 :], back[: chips // 2])
        grad_hidden = turn_back(here, back, lax.ppermute(leave, "mp", SWAP))
    else:
        grad_query, grad_keys, grad_values = finish(stats)
        gathered = lax.all_gather(own, "dp", axis=0, tiled=True).reshape(responses, plen, 2 * width)
        summed = jnp.einsum(
            "rtc,rtk->ck", take_blocks(hidden, all_prompts), gathered, precision=HIGH
        )
        grad_w_key, grad_w_value = summed[:, :width], summed[:, width:]
        terms = jnp.einsum("rtk,ck->rtc", gathered, weights, precision=HIGH)
        numbers = jnp.arange(responses)
        same = all_prompts[:, None] == all_prompts[None, :]
        earlier = jnp.sum(same & (numbers[None, :] < numbers[:, None]), 1)
        hidden_terms = 0.0
        for i in range(responses // PROMPT_COUNT):
            hit = (all_prompts[None, :] == jnp.arange(PROMPT_COUNT)[:, None]) & (earlier[None, :] == i)
            place = jnp.sum(jnp.where(hit, numbers[None, :], 0), -1)
            hidden_terms = hidden_terms + take_blocks(terms, place)
        back = lax.all_to_all(hidden_terms.reshape(chips, rows_own, slice_width), "dp", 0, 0)
        back = back.transpose(1, 0, 2).reshape(rows_own, model)
        grad_hidden = lax.psum_scatter(back, "mp", scatter_dimension=1, tiled=True)
    return (
        result,
        grad_query,
        grad_keys,
        grad_values,
        grad_hidden,
        grad_w_key,
        grad_w_value,
    )


def solution(mesh):
    short = mesh.shape["dp"] == 16 and mesh.shape["mp"] == 2
    in_specs = (P("dp", None),) + (P("dp", "mp"),) * 6 + (P("dp"),) * 2
    out_specs = (P("dp", "mp"),) * 7
    return jax.shard_map(
        functools.partial(per_device, short),
        mesh=mesh,
        in_specs=in_specs,
        out_specs=out_specs,
        check_vma=False,
    )
```

```python
import functools
import math

import jax
import jax.numpy as jnp
from jax import lax
from jax.experimental import pallas as pl
from jax.experimental.pallas import tpu as pltpu
from jax.sharding import PartitionSpec as P

QUERY_HEADS = 40
KEY_VALUE_HEADS = 8
HEAD_SIZE = 128
PROMPT_COUNT = 16
RESPONSE_LENGTH = 256

masked_value = -1e30
HIGH = lax.Precision.HIGH
BOTH = ("dp", "mp")


def pairs_of(target):
    return [
        (c * 2 + m, target(c, m) * 2 + m)
        for c in range(16)
        for m in range(2)
        if target(c, m) is not None
    ]


def along_z(moves):
    return pairs_of(lambda c, m: moves[c >> 2] << 2 | c & 3 if c >> 2 in moves else None)


SECOND = pairs_of(lambda c, m: c ^ (2, 1)[m])
THIRD = pairs_of(lambda c, m: c ^ (1, 2)[m])
ACROSS = [along_z({z: z ^ k for z in range(4)}) for k in range(4)]
MIDDLE = along_z({1: 2, 2: 1})
INWARD = along_z({0: 1, 3: 2})
OUTWARD = along_z({1: 0, 2: 3})
SWAP = [(0, 1), (1, 0)]


def permute(x, pairs):
    return lax.ppermute(x, BOTH, pairs)


def gathered_inner(core):
    return jnp.where(core == 0, jnp.array([0, 2, 1, 3]), jnp.array([0, 1, 2, 3]))


def gathered_order(chip, inner):
    middle = (chip // 4 == 1) | (chip // 4 == 2)
    steps = jnp.where(middle, jnp.array([0, 1, 3, 2]), jnp.array([0, 1, 2, 3]))
    return (chip ^ (steps[:, None] * 4) ^ inner[None, :]).reshape(16)


def scatter_order(chip, core):
    z = chip // 4
    rows = jnp.array([[3, 2, 1, 0], [3, 2, 0, 1], [0, 1, 3, 2], [0, 1, 2, 3]])
    z_order = jnp.sum(jnp.where(jnp.arange(4)[:, None] == z, rows, 0), 0)
    inner = jnp.where(core == 0, jnp.array([3, 1, 2, 0]), jnp.array([3, 2, 1, 0]))
    return (z_order[:, None] * 4 + ((chip & 3) ^ inner)[None, :]).reshape(16)


def reduce_blocks(send, keep):
    part = []
    for k in range(4):
        rows = keep[k].shape[0] // 2
        come = permute(send[k], THIRD)
        passing = keep[k][:rows] + come[:rows]
        part.append(keep[k][rows:] + come[rows:] + permute(passing, SECOND))
    first = permute(part[0], INWARD)
    second = permute(part[1], INWARD)
    third = permute(part[2], INWARD)
    passed = permute(part[0] + first, MIDDLE)
    later = permute(part[1] + second, MIDDLE)
    last = permute(part[2] + passed, OUTWARD)
    return part[3] + third + later + last


def two_terms(x):
    upper = x.astype(jnp.bfloat16)
    return upper, (x - upper.astype(jnp.float32)).astype(jnp.bfloat16)


def dot(a, b, dims):
    return lax.dot_general(a, b, (dims, ((), ())), preferred_element_type=jnp.float32)


def dot_terms(a, b, dims=((1,), (0,))):
    return dot(a[0], b[0], dims) + (dot(a[0], b[1], dims) + dot(a[1], b[0], dims))


def beside(terms):
    return jnp.concatenate(terms, 1)


def halves(x):
    n = x.shape[1] // 2
    return x[:, :n] + x[:, n:]


def dot_rows(a, b):
    rows = jnp.concatenate([beside([b[0], b[0]]), beside([b[1], b[1]])], 0)
    return halves(dot(beside(a), rows, ((1,), (1,))))


def dot_columns(a, b):
    pair = beside(b)
    return halves(dot(beside(a), jnp.concatenate([pair, pair], 0), ((1,), (0,))))


def dot_turned(a, b):
    n = a[0].shape[1]
    out = halves(dot(beside(a), beside(b), ((0,), (0,))))
    return out[:n] + out[n:]


def row_sums(x):
    return dot(beside(two_terms(x)), jnp.ones((2 * x.shape[1], HEAD_SIZE), jnp.bfloat16), ((1,), (0,)))


def three_terms(x):
    first = x.astype(jnp.bfloat16)
    rest = x - first.astype(jnp.float32)
    second = rest.astype(jnp.bfloat16)
    return first, second, (rest - second.astype(jnp.float32)).astype(jnp.bfloat16)


def dot_rows_exact(a, b):
    b = three_terms(b)
    small = dot(beside([a[2], a[0]]), beside([b[0], b[2]]), ((1,), (1,)))
    return dot_rows(a[:2], b[:2]) + small


VMEM_LIMIT = 40 << 20
WHOLE_LIMIT = 32 << 20


def call(kernel, name, grid, in_specs, out_specs, out_shape, scalars=0, limit=VMEM_LIMIT):
    return pl.pallas_call(
        kernel,
        out_shape=[jax.ShapeDtypeStruct(*shape) for shape in out_shape],
        grid_spec=pltpu.PrefetchScalarGridSpec(
            num_scalar_prefetch=scalars, grid=grid, in_specs=in_specs, out_specs=out_specs
        ),
        compiler_params=pltpu.CompilerParams(vmem_limit_bytes=limit),
        name=name,
    )


def call_whole(kernel, name, ins, out_shape, scalars=0):
    vmem = pl.BlockSpec(memory_space=pltpu.VMEM)
    return pl.pallas_call(
        kernel,
        out_shape=[jax.ShapeDtypeStruct(*shape) for shape in out_shape],
        in_specs=[pl.BlockSpec(memory_space=pltpu.SMEM)] * scalars + [vmem] * (len(ins) - scalars),
        out_specs=[vmem] * len(out_shape),
        compiler_params=pltpu.CompilerParams(vmem_limit_bytes=WHOLE_LIMIT),
        name=name,
    )(*ins)


ID_ROWS = 8


def turn_kernel(core, prompt, x, out):
    t = x[...].T
    count, rows, _ = out.shape
    half = rows - ID_ROWS
    for c in range(count):
        own = t[2 * c * half : 2 * (c + 1) * half]
        out[c, :half] = jnp.where(core[0] == 0, own[:half], own[half:])
        out[c, half:] = jnp.full((ID_ROWS, out.shape[2]), prompt[0].astype(jnp.float32))


def turn(core, prompt, hidden, chips):
    rows, model = hidden.shape
    half = model // chips // 2
    (out,) = call(
        turn_kernel,
        "turn",
        (4,),
        [pl.BlockSpec((rows, model // 4), lambda i, *_: (0, i))],
        [pl.BlockSpec((chips // 4, half + ID_ROWS, rows), lambda i, *_: (i, 0, 0))],
        [((chips, half + ID_ROWS, rows), jnp.float32)],
        scalars=2,
    )(core, prompt, hidden)
    return out


def turn_back_kernel(core, own, other, out):
    first = core[0] == 0
    parts = []
    for c in range(own.shape[0]):
        x, y = own[c], other[c]
        parts += [jnp.where(first, x, y), jnp.where(first, y, x)]
    out[...] = jnp.concatenate(parts, 0).T


def turn_back(core, back, come):
    chips, half, rows = back.shape
    steps = chips // 4
    (out,) = call(
        turn_back_kernel,
        "turn_back",
        (steps,),
        [
            pl.BlockSpec((2, half, rows), lambda i, core: (core[0] * steps + i, 0, 0)),
            pl.BlockSpec((2, half, rows), lambda i, core: (i, 0, 0)),
        ],
        [pl.BlockSpec((rows, 4 * half), lambda i, *_: (0, i))],
        [((rows, chips * half), jnp.float32)],
        scalars=1,
    )(core, back, come)
    return out


def split_kernel(core, key, value, out):
    depth, width = key.shape
    half = depth // 2
    first = core[0] == 0
    for start, ref in ((0, key), (width, value)):
        x, y = ref[:half], ref[half:]
        for row, part in ((0, jnp.where(first, x, y)), (half, jnp.where(first, y, x))):
            upper, lower = two_terms(part)
            for place, term in enumerate((upper, upper, lower)):
                top = place * depth + row
                out[top : top + half, start : start + width] = term


def split_weights(core, key, value):
    shape = (3 * key.shape[0], 2 * key.shape[1])
    (out,) = call_whole(
        split_kernel, "split_weights", [core, key, value], [(shape, jnp.bfloat16)], scalars=1
    )
    return out


def project_kernel(index, own, other, weights, send, keep):
    half = own.shape[1] - ID_ROWS
    both = jnp.concatenate(
        [beside([ref[index[q], :half] for q in range(4)]) for ref in (own, other)], 0
    )
    upper, lower = two_terms(both)
    terms = dot(jnp.concatenate([upper, lower, upper], 0).T, weights[...], ((1,), (0,)))
    count = send.shape[0]
    send[...] = terms[:count]
    keep[...] = terms[count:]


def project(index, own, other, weights):
    shape = ((2 * own.shape[2], weights.shape[1]), jnp.float32)
    return call_whole(
        project_kernel, "project", [index, own, other, weights], [shape] * 2, scalars=1
    )


def weight_times(weights, blocks):
    depth = weights.shape[0] // 3
    terms = weights[:depth], weights[2 * depth :]
    out = []
    for q in range(0, len(blocks), 2):
        x = two_terms(jnp.concatenate([blocks[q][...], blocks[q + 1][...]], 0))
        out.append(dot_terms(terms, x, ((1,), (1,))))
    return out


def hidden_part_kernel(place, *refs):
    blocks, weights, (keep, give) = refs[:-3], refs[-3], refs[-2:]
    half, plen = keep.shape[1:]
    for q, part in enumerate(weight_times(weights, blocks)):
        for i in range(2):
            piece = part[:, i * plen : (i + 1) * plen]
            keep[place[2 * q + i]] = piece[:half]
            give[place[2 * q + i]] = piece[half:]


def hidden_part(place, blocks, weights):
    shape = ((len(blocks), weights.shape[0] // 6, blocks[0].shape[0]), jnp.float32)
    return call_whole(
        hidden_part_kernel, "hidden_part", [place, *blocks, weights], [shape] * 2, scalars=1
    )


def hidden_last_kernel(place, keep_in, give_in, *refs):
    blocks, weights, (keep, give) = refs[:-3], refs[-3], refs[-2:]
    half, plen = keep.shape[1:]
    (part,) = weight_times(weights, blocks)
    for i in range(2):
        keep[place[i]] = keep_in[i]
        give[place[i]] = give_in[i]
        piece = part[:, i * plen : (i + 1) * plen]
        keep[place[2 + i]] = piece[:half]
        give[place[2 + i]] = piece[half:]


def hidden_last(place, keep, give, blocks, weights):
    shape = ((4,) + keep.shape[1:], jnp.float32)
    return call_whole(
        hidden_last_kernel,
        "hidden_last",
        [place, keep, give, *blocks, weights],
        [shape] * 2,
        scalars=1,
    )


def assemble_kernel(listed, *refs):
    keep, come, out = refs[:4], refs[4:8], refs[8]
    for k in range(4):
        for i in range(4):
            out[listed[4 * k + i]] = keep[k][i] + come[k][i]


def assemble(listed, keep, come):
    shape = ((16,) + keep[0].shape[1:], jnp.float32)
    (out,) = call_whole(assemble_kernel, "assemble", [listed, *keep, *come], [shape], scalars=1)
    return out


def weight_grad_kernel(listed, core, own, other, *refs):
    blocks, outs = refs[:-2], refs[-2:]
    half = own.shape[1] - ID_ROWS
    width = outs[0].shape[1]
    total = None
    for q in range(0, len(blocks), 4):
        x = jnp.concatenate(
            [beside([ref[listed[q + i], :half] for i in range(4)]) for ref in (own, other)], 0
        )
        g = jnp.concatenate([ref[...] for ref in blocks[q : q + 4]], 0)
        term = dot_terms(two_terms(x), two_terms(g))
        total = term if total is None else total + term
    x, y = total[:half], total[half:]
    first = core[0] == 0
    for row, part in ((0, jnp.where(first, x, y)), (half, jnp.where(first, y, x))):
        for out, start in zip(outs, (0, width)):
            out[row : row + half] = part[:, start : start + width]


def weight_grad(listed, core, own, other, blocks):
    plen, columns = blocks[0].shape
    shape = ((2 * (own.shape[1] - ID_ROWS), columns // 2), jnp.float32)
    return call_whole(
        weight_grad_kernel,
        "weight_grad",
        [listed, core, own, other, *blocks],
        [shape] * 2,
        scalars=2,
    )


SCALE = 1.0 / math.sqrt(HEAD_SIZE)
PER_GROUP = QUERY_HEADS // KEY_VALUE_HEADS


def stack(ref):
    size = ref.shape[1] // PER_GROUP
    return jnp.concatenate([ref[:, h * size : (h + 1) * size] for h in range(PER_GROUP)], 0)


def unstack(ref, x):
    rows, size = ref.shape[0], ref.shape[1] // PER_GROUP
    for h in range(PER_GROUP):
        ref[:, h * size : (h + 1) * size] = x[h * rows : (h + 1) * rows]


def save_columns(ref, first, second):
    rows = ref.shape[0]
    lane = lax.broadcasted_iota(jnp.int32, ref.shape, 1)
    out = jnp.zeros(ref.shape, jnp.float32)
    for start, column in ((0, first), (8, second)):
        for h in range(PER_GROUP):
            out = jnp.where(lane == start + h, column[h * rows : (h + 1) * rows], out)
    ref[...] = out


def load_column(ref, start):
    return jnp.concatenate([ref[:, start + h : start + h + 1] for h in range(PER_GROUP)], 0)


def row_number(shape, rows):
    return lax.broadcasted_iota(jnp.int32, shape, 0) % rows


def own_scores(length, query, keys, rows):
    scores = dot_rows_exact(query, keys) * SCALE
    j = lax.broadcasted_iota(jnp.int32, scores.shape, 1)
    return jnp.where((j <= row_number(scores.shape, rows)) & (j < length), scores, masked_value)


def open_kernel(length, q, g, k, v, total, stats, q1, q2, q3, g1, g2):
    query_terms = three_terms(stack(q))
    for ref, term in zip((q1, q2, q3), query_terms):
        unstack(ref, term)
    upstream = stack(g)
    upstream = jnp.where(row_number(upstream.shape, q.shape[0]) < length[0], upstream, 0.0)
    for ref, term in zip((g1, g2), two_terms(upstream)):
        unstack(ref, term)
    scores = own_scores(length[0], query_terms, k[...], q.shape[0])
    top = jnp.max(scores, -1, keepdims=True)
    expo = jnp.exp(scores - top)
    unstack(total, dot_columns(two_terms(expo), two_terms(v[...])))
    save_columns(stats, top, jnp.sum(expo, -1, keepdims=True))


def close_kernel(length, q1, q2, q3, g, g1, g2, kp, vp, total, stats, out, grad_scores, stats_out, gk, gv):
    query_terms = stack(q1), stack(q2), stack(q3)
    plen = kp.shape[0]
    scores = dot_rows_exact(query_terms, kp[...]) * SCALE
    before = load_column(stats, 0)
    top = jnp.maximum(before, jnp.max(scores, -1, keepdims=True))
    weight = jnp.exp(before - top)
    expo = jnp.exp(scores - top)
    denominator = weight * load_column(stats, 8) + row_sums(expo)
    inverse = 1.0 / denominator
    prob = expo * (inverse if plen == HEAD_SIZE else inverse[:, :1])
    prob_terms, value_terms = two_terms(prob), two_terms(vp[...])
    result = (weight * inverse) * stack(total) + dot_columns(prob_terms, value_terms)
    result = jnp.where(row_number(result.shape, g.shape[0]) < length[0], result, 0.0)
    upstream_terms = stack(g1), stack(g2)
    inner = row_sums(stack(g) * result)
    inner_here = inner if plen == HEAD_SIZE else inner[:, :1]
    grad = prob * (dot_rows(upstream_terms, value_terms) - inner_here) * SCALE
    unstack(out, result)
    unstack(grad_scores, grad)
    save_columns(stats_out, top + jnp.log(denominator), inner)
    gk[...] = dot_turned(two_terms(grad), query_terms[:2])
    gv[...] = dot_turned(prob_terms, upstream_terms)


def finish_kernel(length, q1, q2, q3, g1, g2, k, v, kp, grad_scores, stats, gq, gk, gv):
    query_terms, keys = (stack(q1), stack(q2), stack(q3)), k[...]
    prob = jnp.exp(own_scores(length[0], query_terms, keys, q1.shape[0]) - load_column(stats, 0))
    upstream_terms = stack(g1), stack(g2)
    grad = prob * (dot_rows(upstream_terms, two_terms(v[...])) - load_column(stats, 8)) * SCALE
    grad_terms = two_terms(grad)
    prompt_part = dot_columns(two_terms(stack(grad_scores)), two_terms(kp[...]))
    unstack(gq, prompt_part + dot_columns(grad_terms, two_terms(keys)))
    gk[...] = dot_turned(grad_terms, query_terms[:2])
    gv[...] = dot_turned(two_terms(prob), upstream_terms)


def attention(kernel, name, groups, length, ins, outs):
    return call(
        kernel,
        name,
        (groups,),
        [
            pl.BlockSpec((x.shape[0], size), lambda i, *_, skip=skip: (0, skip + i))
            for x, size, skip in ins
        ],
        [pl.BlockSpec((rows, size), lambda i, *_: (0, i)) for rows, size, _ in outs],
        [((rows, groups * size), kind) for rows, size, kind in outs],
        scalars=1,
    )(length, *(x for x, _, _ in ins))


def take_blocks(x, index):
    return jnp.stack(
        [lax.dynamic_index_in_dim(x, index[j], keepdims=False) for j in range(index.shape[0])]
    )


def take_small(table, index):
    hit = index[..., None] == jnp.arange(table.shape[0])
    return jnp.sum(jnp.where(hit, table, 0), -1)


def per_device(
    short,
    prompt_hidden,
    key_weight,
    value_weight,
    queries,
    keys_resp,
    response_value_rows,
    grad_out,
    resp_prompt,
    resp_len,
):
    chips = lax.axis_size("dp")
    chip, core = lax.axis_index("dp"), lax.axis_index("mp")
    rows_own, model = prompt_hidden.shape
    slice_width = model // chips
    width = key_weight.shape[1]
    groups = width // HEAD_SIZE
    plen = rows_own * chips // PROMPT_COUNT
    tokens = queries.shape[0]
    responses = tokens * chips // RESPONSE_LENGTH
    assert tokens == RESPONSE_LENGTH
    short = short and responses == PROMPT_COUNT
    here = core.astype(jnp.int32)[None]
    wide = PER_GROUP * HEAD_SIZE

    if short:
        mine = lax.all_to_all(turn(here, resp_prompt, prompt_hidden, chips), "dp", 0, 0)
        weight_terms = split_weights(here, key_weight, value_weight)
    else:
        all_prompts = lax.all_gather(resp_prompt, "dp", axis=0, tiled=True)
        hidden = lax.all_to_all(
            prompt_hidden.reshape(rows_own, chips, slice_width).transpose(1, 0, 2), "dp", 0, 0
        )
        hidden = hidden.reshape(PROMPT_COUNT, plen, slice_width)
        weights = jnp.concatenate([key_weight, value_weight], 1)

    whole_heads, one_head = (tokens, wide, jnp.float32), (tokens, HEAD_SIZE, jnp.float32)
    total, stats, *kept = attention(
        open_kernel,
        "open",
        groups,
        resp_len,
        [
            (queries, wide, 0),
            (grad_out, wide, 0),
            (keys_resp, HEAD_SIZE, 0),
            (response_value_rows, HEAD_SIZE, 0),
        ],
        [whole_heads, one_head] + [(tokens, wide, jnp.bfloat16)] * 5,
    )

    if short:
        mine, weight_terms, total, stats, kept = lax.optimization_barrier(
            (mine, weight_terms, total, stats, kept)
        )
        all_prompts = mine[:, slice_width // 2, 0].astype(jnp.int32)
        other = lax.ppermute(mine, "mp", SWAP)
        listed = take_small(all_prompts, scatter_order(chip, core))
        pairs = [project(listed[4 * k : 4 * k + 4], mine, other, weight_terms) for k in range(4)]
        prompt_rows = reduce_blocks([pair[0] for pair in pairs], [pair[1] for pair in pairs])
    else:
        terms = jnp.einsum("rtc,ck->rtk", take_blocks(hidden, all_prompts), weights, precision=HIGH)
        prompt_rows = lax.psum_scatter(
            terms.reshape(responses * plen, 2 * width), "dp", scatter_dimension=0, tiled=True
        )

    query_terms = [(x, wide, 0) for x in kept[:3]]
    upstream_terms = [(x, wide, 0) for x in kept[3:]]
    prompt_keys = (prompt_rows, HEAD_SIZE, 0)
    result, grad_scores, stats, own_k, own_v = attention(
        close_kernel,
        "close",
        groups,
        resp_len,
        query_terms
        + [(grad_out, wide, 0)]
        + upstream_terms
        + [prompt_keys, (prompt_rows, HEAD_SIZE, groups), (total, wide, 0), (stats, HEAD_SIZE, 0)],
        [whole_heads, (tokens, PER_GROUP * plen, jnp.float32), one_head]
        + [(plen, HEAD_SIZE, jnp.float32)] * 2,
    )

    def finish(stats):
        own_ins = [(keys_resp, HEAD_SIZE, 0), (response_value_rows, HEAD_SIZE, 0), prompt_keys]
        kept_ins = [(grad_scores, PER_GROUP * plen, 0), (stats, HEAD_SIZE, 0)]
        return attention(
            finish_kernel,
            "finish",
            groups,
            resp_len,
            query_terms + upstream_terms + own_ins + kept_ins,
            [whole_heads] + [one_head] * 2,
        )

    own = jnp.concatenate([own_k, own_v], 1)
    if short:
        place = gathered_inner(core)
        listed = take_small(all_prompts, gathered_order(chip, jnp.arange(4)))
        far = [own, permute(own, ACROSS[1])]
        ahead = permute(own, MIDDLE)
        near, third, both = [permute(own, SECOND)], [permute(own, THIRD)], []

        def group(k):
            return [far[k], near[k], third[k], both[k]]

        far[1], ahead, near[0], third[0] = lax.optimization_barrier(
            (far[1], ahead, near[0], third[0])
        )
        beyond = permute(far[1], MIDDLE)
        come = permute(ahead, OUTWARD)
        near.append(permute(far[1], SECOND))
        third.append(permute(far[1], THIRD))
        both.append(permute(near[0], THIRD))
        beyond, come, near[1] = lax.optimization_barrier((beyond, come, near[1]))
        far.append(ahead + come)
        come = permute(beyond, OUTWARD)
        near.append(permute(far[2], SECOND))
        third.append(permute(far[2], THIRD))
        both.append(permute(near[1], THIRD))
        done = hidden_part(place, group(0), weight_terms)
        come, near[2], done = lax.optimization_barrier((come, near[2], done))
        far.append(beyond + come)
        near.append(permute(far[3], SECOND))
        third.append(permute(far[3], THIRD))
        both.append(permute(near[2], THIRD))
        parts = [done]
        near[3], done = lax.optimization_barrier(
            (near[3], hidden_part(place, group(1), weight_terms))
        )
        both.append(permute(near[3], THIRD))
        parts.append(done)
        parts.append(hidden_part(place, group(2), weight_terms))
        come = [lax.ppermute(give, "mp", SWAP) for _, give in parts]
        pair = hidden_part(jnp.arange(2), [far[3], near[3]], weight_terms)
        third[3], both[3], parts, come, pair, stats_late = lax.optimization_barrier(
            (third[3], both[3], parts, come, pair, stats)
        )
        parts.append(hidden_last(place, *pair, [third[3], both[3]], weight_terms))
        come.append(lax.ppermute(parts[3][1], "mp", SWAP))
        back = lax.all_to_all(assemble(listed, [x for x, _ in parts], come), "dp", 0, 0)

        order = take_small(all_prompts, gathered_order(chip, place))
        gathered = [x for k in range(4) for x in group(k)]
        grad_w_key, grad_w_value = weight_grad(order, here, mine, other, gathered)
        back, grad_w_key, grad_w_value, state = lax.optimization_barrier(
            (back, grad_w_key, grad_w_value, finish(stats_late))
        )
        grad_query, grad_keys, grad_values = state
        leave = jnp.where(core == 0, back[chips // 2 :], back[: chips // 2])
        grad_hidden = turn_back(here, back, lax.ppermute(leave, "mp", SWAP))
    else:
        grad_query, grad_keys, grad_values = finish(stats)
        gathered = lax.all_gather(own, "dp", axis=0, tiled=True).reshape(responses, plen, 2 * width)
        summed = jnp.einsum(
            "rtc,rtk->ck", take_blocks(hidden, all_prompts), gathered, precision=HIGH
        )
        grad_w_key, grad_w_value = summed[:, :width], summed[:, width:]
        terms = jnp.einsum("rtk,ck->rtc", gathered, weights, precision=HIGH)
        numbers = jnp.arange(responses)
        same = all_prompts[:, None] == all_prompts[None, :]
        earlier = jnp.sum(same & (numbers[None, :] < numbers[:, None]), 1)
        hidden_terms = 0.0
        for i in range(responses // PROMPT_COUNT):
            hit = (all_prompts[None, :] == jnp.arange(PROMPT_COUNT)[:, None]) & (earlier[None, :] == i)
            place = jnp.sum(jnp.where(hit, numbers[None, :], 0), -1)
            hidden_terms = hidden_terms + take_blocks(terms, place)
        back = lax.all_to_all(hidden_terms.reshape(chips, rows_own, slice_width), "dp", 0, 0)
        back = back.transpose(1, 0, 2).reshape(rows_own, model)
        grad_hidden = lax.psum_scatter(back, "mp", scatter_dimension=1, tiled=True)
    return (
        result,
        grad_query,
        grad_keys,
        grad_values,
        grad_hidden,
        grad_w_key,
        grad_w_value,
    )


def solution(mesh):
    short = mesh.shape["dp"] == 16 and mesh.shape["mp"] == 2
    in_specs = (P("dp", None),) + (P("dp", "mp"),) * 6 + (P("dp"),) * 2
    out_specs = (P("dp", "mp"),) * 7
    return jax.shard_map(
        functools.partial(per_device, short),
        mesh=mesh,
        in_specs=in_specs,
        out_specs=out_specs,
        check_vma=False,
    )
```

```python
import functools
import math

import jax
import jax.numpy as jnp
from jax import lax
from jax.experimental import pallas as pl
from jax.experimental.pallas import tpu as pltpu
from jax.sharding import PartitionSpec as P

QUERY_HEADS = 40
KEY_VALUE_HEADS = 8
HEAD_SIZE = 128
PROMPT_COUNT = 16
RESPONSE_LENGTH = 256

masked_value = -1e30
HIGH = lax.Precision.HIGH
BOTH = ("dp", "mp")


def pairs_of(target):
    return [
        (c * 2 + m, target(c, m) * 2 + m)
        for c in range(16)
        for m in range(2)
        if target(c, m) is not None
    ]


def along_z(moves):
    return pairs_of(lambda c, m: moves[c >> 2] << 2 | c & 3 if c >> 2 in moves else None)


SECOND = pairs_of(lambda c, m: c ^ (2, 1)[m])
THIRD = pairs_of(lambda c, m: c ^ (1, 2)[m])
ACROSS = [along_z({z: z ^ k for z in range(4)}) for k in range(4)]
MIDDLE = along_z({1: 2, 2: 1})
INWARD = along_z({0: 1, 3: 2})
OUTWARD = along_z({1: 0, 2: 3})
SWAP = [(0, 1), (1, 0)]


def permute(x, pairs):
    return lax.ppermute(x, BOTH, pairs)


def gathered_inner(core):
    return jnp.where(core == 0, jnp.array([0, 2, 1, 3]), jnp.array([0, 1, 2, 3]))


def gathered_order(chip, inner):
    middle = (chip // 4 == 1) | (chip // 4 == 2)
    steps = jnp.where(middle, jnp.array([0, 1, 3, 2]), jnp.array([0, 1, 2, 3]))
    return (chip ^ (steps[:, None] * 4) ^ inner[None, :]).reshape(16)


def scatter_order(chip, core):
    z = chip // 4
    rows = jnp.array([[3, 2, 1, 0], [3, 2, 0, 1], [0, 1, 3, 2], [0, 1, 2, 3]])
    z_order = jnp.sum(jnp.where(jnp.arange(4)[:, None] == z, rows, 0), 0)
    inner = jnp.where(core == 0, jnp.array([3, 1, 2, 0]), jnp.array([3, 2, 1, 0]))
    return (z_order[:, None] * 4 + ((chip & 3) ^ inner)[None, :]).reshape(16)


def reduce_blocks(send, keep):
    part = []
    for k in range(4):
        rows = keep[k].shape[0] // 2
        come = permute(send[k], THIRD)
        passing = keep[k][:rows] + come[:rows]
        part.append(keep[k][rows:] + come[rows:] + permute(passing, SECOND))
    first = permute(part[0], INWARD)
    second = permute(part[1], INWARD)
    third = permute(part[2], INWARD)
    passed = permute(part[0] + first, MIDDLE)
    later = permute(part[1] + second, MIDDLE)
    last = permute(part[2] + passed, OUTWARD)
    return part[3] + third + later + last


def two_terms(x):
    upper = x.astype(jnp.bfloat16)
    return upper, (x - upper.astype(jnp.float32)).astype(jnp.bfloat16)


def dot(a, b, dims):
    return lax.dot_general(a, b, (dims, ((), ())), preferred_element_type=jnp.float32)


def dot_terms(a, b, dims=((1,), (0,))):
    return dot(a[0], b[0], dims) + (dot(a[0], b[1], dims) + dot(a[1], b[0], dims))


def beside(terms):
    return jnp.concatenate(terms, 1)


def halves(x):
    n = x.shape[1] // 2
    return x[:, :n] + x[:, n:]


def dot_rows(a, b):
    rows = jnp.concatenate([beside([b[0], b[0]]), beside([b[1], b[1]])], 0)
    return halves(dot(beside(a), rows, ((1,), (1,))))


def dot_columns(a, b):
    pair = beside(b)
    return halves(dot(beside(a), jnp.concatenate([pair, pair], 0), ((1,), (0,))))


def dot_turned(a, b):
    n = a[0].shape[1]
    out = halves(dot(beside(a), beside(b), ((0,), (0,))))
    return out[:n] + out[n:]


def row_sums(x):
    return dot(beside(two_terms(x)), jnp.ones((2 * x.shape[1], HEAD_SIZE), jnp.bfloat16), ((1,), (0,)))


def three_terms(x):
    first = x.astype(jnp.bfloat16)
    rest = x - first.astype(jnp.float32)
    second = rest.astype(jnp.bfloat16)
    return first, second, (rest - second.astype(jnp.float32)).astype(jnp.bfloat16)


def dot_rows_exact(a, b):
    b = three_terms(b)
    small = dot(beside([a[2], a[0]]), beside([b[0], b[2]]), ((1,), (1,)))
    return dot_rows(a[:2], b[:2]) + small


VMEM_LIMIT = 40 << 20
WHOLE_LIMIT = 32 << 20


def call(kernel, name, grid, in_specs, out_specs, out_shape, scalars=0, limit=VMEM_LIMIT):
    return pl.pallas_call(
        kernel,
        out_shape=[jax.ShapeDtypeStruct(*shape) for shape in out_shape],
        grid_spec=pltpu.PrefetchScalarGridSpec(
            num_scalar_prefetch=scalars, grid=grid, in_specs=in_specs, out_specs=out_specs
        ),
        compiler_params=pltpu.CompilerParams(vmem_limit_bytes=limit),
        name=name,
    )


def call_whole(kernel, name, ins, out_shape, scalars=0):
    vmem = pl.BlockSpec(memory_space=pltpu.VMEM)
    return pl.pallas_call(
        kernel,
        out_shape=[jax.ShapeDtypeStruct(*shape) for shape in out_shape],
        in_specs=[pl.BlockSpec(memory_space=pltpu.SMEM)] * scalars + [vmem] * (len(ins) - scalars),
        out_specs=[vmem] * len(out_shape),
        compiler_params=pltpu.CompilerParams(vmem_limit_bytes=WHOLE_LIMIT),
        name=name,
    )(*ins)


ID_ROWS = 8


def turn_kernel(core, prompt, x, out):
    t = x[...].T
    count, rows, _ = out.shape
    half = rows - ID_ROWS
    for c in range(count):
        own = t[2 * c * half : 2 * (c + 1) * half]
        out[c, :half] = jnp.where(core[0] == 0, own[:half], own[half:])
        out[c, half:] = jnp.full((ID_ROWS, out.shape[2]), prompt[0].astype(jnp.float32))


def turn(core, prompt, hidden, chips):
    rows, model = hidden.shape
    half = model // chips // 2
    (out,) = call(
        turn_kernel,
        "turn",
        (4,),
        [pl.BlockSpec((rows, model // 4), lambda i, *_: (0, i))],
        [pl.BlockSpec((chips // 4, half + ID_ROWS, rows), lambda i, *_: (i, 0, 0))],
        [((chips, half + ID_ROWS, rows), jnp.float32)],
        scalars=2,
    )(core, prompt, hidden)
    return out


def turn_back_kernel(core, own, other, out):
    first = core[0] == 0
    parts = []
    for c in range(own.shape[0]):
        x, y = own[c], other[c]
        parts += [jnp.where(first, x, y), jnp.where(first, y, x)]
    out[...] = jnp.concatenate(parts, 0).T


def turn_back(core, back, come):
    chips, half, rows = back.shape
    steps = chips // 4
    (out,) = call(
        turn_back_kernel,
        "turn_back",
        (steps,),
        [
            pl.BlockSpec((2, half, rows), lambda i, core: (core[0] * steps + i, 0, 0)),
            pl.BlockSpec((2, half, rows), lambda i, core: (i, 0, 0)),
        ],
        [pl.BlockSpec((rows, 4 * half), lambda i, *_: (0, i))],
        [((rows, chips * half), jnp.float32)],
        scalars=1,
    )(core, back, come)
    return out


def split_kernel(core, key, value, out):
    depth, width = key.shape
    half = depth // 2
    first = core[0] == 0
    for start, ref in ((0, key), (width, value)):
        x, y = ref[:half], ref[half:]
        for row, part in ((0, jnp.where(first, x, y)), (half, jnp.where(first, y, x))):
            upper, lower = two_terms(part)
            for place, term in enumerate((upper, upper, lower)):
                top = place * depth + row
                out[top : top + half, start : start + width] = term


def split_weights(core, key, value):
    shape = (3 * key.shape[0], 2 * key.shape[1])
    (out,) = call_whole(
        split_kernel, "split_weights", [core, key, value], [(shape, jnp.bfloat16)], scalars=1
    )
    return out


def project_kernel(index, own, other, weights, send, keep):
    half = own.shape[1] - ID_ROWS
    both = jnp.concatenate(
        [beside([ref[index[q], :half] for q in range(4)]) for ref in (own, other)], 0
    )
    upper, lower = two_terms(both)
    terms = dot(jnp.concatenate([upper, lower, upper], 0).T, weights[...], ((1,), (0,)))
    count = send.shape[0]
    send[...] = terms[:count]
    keep[...] = terms[count:]


def project(index, own, other, weights):
    shape = ((2 * own.shape[2], weights.shape[1]), jnp.float32)
    return call_whole(
        project_kernel, "project", [index, own, other, weights], [shape] * 2, scalars=1
    )


def weight_times(weights, blocks):
    depth = weights.shape[0] // 3
    terms = weights[:depth], weights[2 * depth :]
    out = []
    for q in range(0, len(blocks), 2):
        x = two_terms(jnp.concatenate([blocks[q][...], blocks[q + 1][...]], 0))
        out.append(dot_terms(terms, x, ((1,), (1,))))
    return out


def hidden_part_kernel(place, *refs):
    blocks, weights, (keep, give) = refs[:-3], refs[-3], refs[-2:]
    half, plen = keep.shape[1:]
    for q, part in enumerate(weight_times(weights, blocks)):
        for i in range(2):
            piece = part[:, i * plen : (i + 1) * plen]
            keep[place[2 * q + i]] = piece[:half]
            give[place[2 * q + i]] = piece[half:]


def hidden_part(place, blocks, weights):
    shape = ((len(blocks), weights.shape[0] // 6, blocks[0].shape[0]), jnp.float32)
    return call_whole(
        hidden_part_kernel, "hidden_part", [place, *blocks, weights], [shape] * 2, scalars=1
    )


def hidden_last_kernel(place, keep_in, give_in, *refs):
    blocks, weights, (keep, give) = refs[:-3], refs[-3], refs[-2:]
    half, plen = keep.shape[1:]
    (part,) = weight_times(weights, blocks)
    for i in range(2):
        keep[place[i]] = keep_in[i]
        give[place[i]] = give_in[i]
        piece = part[:, i * plen : (i + 1) * plen]
        keep[place[2 + i]] = piece[:half]
        give[place[2 + i]] = piece[half:]


def hidden_last(place, keep, give, blocks, weights):
    shape = ((4,) + keep.shape[1:], jnp.float32)
    return call_whole(
        hidden_last_kernel,
        "hidden_last",
        [place, keep, give, *blocks, weights],
        [shape] * 2,
        scalars=1,
    )


def assemble_kernel(listed, *refs):
    keep, come, out = refs[:4], refs[4:8], refs[8]
    for k in range(4):
        for i in range(4):
            out[listed[4 * k + i]] = keep[k][i] + come[k][i]


def assemble(listed, keep, come):
    shape = ((16,) + keep[0].shape[1:], jnp.float32)
    (out,) = call_whole(assemble_kernel, "assemble", [listed, *keep, *come], [shape], scalars=1)
    return out


def weight_grad_kernel(listed, core, own, other, *refs):
    blocks, outs = refs[:-2], refs[-2:]
    half = own.shape[1] - ID_ROWS
    width = outs[0].shape[1]
    total = None
    for q in range(0, len(blocks), 4):
        x = jnp.concatenate(
            [beside([ref[listed[q + i], :half] for i in range(4)]) for ref in (own, other)], 0
        )
        g = jnp.concatenate([ref[...] for ref in blocks[q : q + 4]], 0)
        term = dot_terms(two_terms(x), two_terms(g))
        total = term if total is None else total + term
    x, y = total[:half], total[half:]
    first = core[0] == 0
    for row, part in ((0, jnp.where(first, x, y)), (half, jnp.where(first, y, x))):
        for out, start in zip(outs, (0, width)):
            out[row : row + half] = part[:, start : start + width]


def weight_grad(listed, core, own, other, blocks):
    plen, columns = blocks[0].shape
    shape = ((2 * (own.shape[1] - ID_ROWS), columns // 2), jnp.float32)
    return call_whole(
        weight_grad_kernel,
        "weight_grad",
        [listed, core, own, other, *blocks],
        [shape] * 2,
        scalars=2,
    )


SCALE = 1.0 / math.sqrt(HEAD_SIZE)
PER_GROUP = QUERY_HEADS // KEY_VALUE_HEADS


def stack(ref):
    size = ref.shape[1] // PER_GROUP
    return jnp.concatenate([ref[:, h * size : (h + 1) * size] for h in range(PER_GROUP)], 0)


def unstack(ref, x):
    rows, size = ref.shape[0], ref.shape[1] // PER_GROUP
    for h in range(PER_GROUP):
        ref[:, h * size : (h + 1) * size] = x[h * rows : (h + 1) * rows]


def save_columns(ref, first, second):
    rows = ref.shape[0]
    lane = lax.broadcasted_iota(jnp.int32, ref.shape, 1)
    out = jnp.zeros(ref.shape, jnp.float32)
    for start, column in ((0, first), (8, second)):
        for h in range(PER_GROUP):
            out = jnp.where(lane == start + h, column[h * rows : (h + 1) * rows], out)
    ref[...] = out


def load_column(ref, start):
    return jnp.concatenate([ref[:, start + h : start + h + 1] for h in range(PER_GROUP)], 0)


def row_number(shape, rows):
    return lax.broadcasted_iota(jnp.int32, shape, 0) % rows


def own_scores(length, query, keys, rows):
    scores = dot_rows_exact(query, keys) * SCALE
    j = lax.broadcasted_iota(jnp.int32, scores.shape, 1)
    return jnp.where((j <= row_number(scores.shape, rows)) & (j < length), scores, masked_value)


def open_kernel(length, q, g, k, v, total, stats, q1, q2, q3, g1, g2):
    query_terms = three_terms(stack(q))
    for ref, term in zip((q1, q2, q3), query_terms):
        unstack(ref, term)
    upstream = stack(g)
    upstream = jnp.where(row_number(upstream.shape, q.shape[0]) < length[0], upstream, 0.0)
    for ref, term in zip((g1, g2), two_terms(upstream)):
        unstack(ref, term)
    scores = own_scores(length[0], query_terms, k[...], q.shape[0])
    top = jnp.max(scores, -1, keepdims=True)
    expo = jnp.exp(scores - top)
    unstack(total, dot_columns(two_terms(expo), two_terms(v[...])))
    save_columns(stats, top, jnp.sum(expo, -1, keepdims=True))


def close_kernel(length, q1, q2, q3, g, g1, g2, kp, vp, total, stats, out, grad_scores, stats_out, gk, gv):
    query_terms = stack(q1), stack(q2), stack(q3)
    plen = kp.shape[0]
    scores = dot_rows_exact(query_terms, kp[...]) * SCALE
    before = load_column(stats, 0)
    top = jnp.maximum(before, jnp.max(scores, -1, keepdims=True))
    weight = jnp.exp(before - top)
    expo = jnp.exp(scores - top)
    denominator = weight * load_column(stats, 8) + row_sums(expo)
    inverse = 1.0 / denominator
    prob = expo * (inverse if plen == HEAD_SIZE else inverse[:, :1])
    prob_terms, value_terms = two_terms(prob), two_terms(vp[...])
    result = (weight * inverse) * stack(total) + dot_columns(prob_terms, value_terms)
    result = jnp.where(row_number(result.shape, g.shape[0]) < length[0], result, 0.0)
    upstream_terms = stack(g1), stack(g2)
    inner = row_sums(stack(g) * result)
    inner_here = inner if plen == HEAD_SIZE else inner[:, :1]
    grad = prob * (dot_rows(upstream_terms, value_terms) - inner_here) * SCALE
    unstack(out, result)
    unstack(grad_scores, grad)
    save_columns(stats_out, top + jnp.log(denominator), inner)
    gk[...] = dot_turned(two_terms(grad), query_terms[:2])
    gv[...] = dot_turned(prob_terms, upstream_terms)


def finish_kernel(length, q1, q2, q3, g1, g2, k, v, kp, grad_scores, stats, gq, gk, gv):
    query_terms, keys = (stack(q1), stack(q2), stack(q3)), k[...]
    prob = jnp.exp(own_scores(length[0], query_terms, keys, q1.shape[0]) - load_column(stats, 0))
    upstream_terms = stack(g1), stack(g2)
    grad = prob * (dot_rows(upstream_terms, two_terms(v[...])) - load_column(stats, 8)) * SCALE
    grad_terms = two_terms(grad)
    prompt_part = dot_columns(two_terms(stack(grad_scores)), two_terms(kp[...]))
    unstack(gq, prompt_part + dot_columns(grad_terms, two_terms(keys)))
    gk[...] = dot_turned(grad_terms, query_terms[:2])
    gv[...] = dot_turned(two_terms(prob), upstream_terms)


def attention(kernel, name, groups, length, ins, outs):
    return call(
        kernel,
        name,
        (groups,),
        [
            pl.BlockSpec((x.shape[0], size), lambda i, *_, skip=skip: (0, skip + i))
            for x, size, skip in ins
        ],
        [pl.BlockSpec((rows, size), lambda i, *_: (0, i)) for rows, size, _ in outs],
        [((rows, groups * size), kind) for rows, size, kind in outs],
        scalars=1,
    )(length, *(x for x, _, _ in ins))


def take_blocks(x, index):
    return jnp.stack(
        [lax.dynamic_index_in_dim(x, index[j], keepdims=False) for j in range(index.shape[0])]
    )


def take_small(table, index):
    hit = index[..., None] == jnp.arange(table.shape[0])
    return jnp.sum(jnp.where(hit, table, 0), -1)


def per_device(
    short,
    prompt_hidden,
    key_weight,
    value_weight,
    queries,
    keys_resp,
    response_value_rows,
    grad_out,
    resp_prompt,
    resp_len,
):
    chips = lax.axis_size("dp")
    chip, core = lax.axis_index("dp"), lax.axis_index("mp")
    rows_own, model = prompt_hidden.shape
    slice_width = model // chips
    width = key_weight.shape[1]
    groups = width // HEAD_SIZE
    plen = rows_own * chips // PROMPT_COUNT
    tokens = queries.shape[0]
    responses = tokens * chips // RESPONSE_LENGTH
    assert tokens == RESPONSE_LENGTH
    short = short and responses == PROMPT_COUNT
    here = core.astype(jnp.int32)[None]
    wide = PER_GROUP * HEAD_SIZE

    if short:
        mine = lax.all_to_all(turn(here, resp_prompt, prompt_hidden, chips), "dp", 0, 0)
        weight_terms = split_weights(here, key_weight, value_weight)
    else:
        all_prompts = lax.all_gather(resp_prompt, "dp", axis=0, tiled=True)
        hidden = lax.all_to_all(
            prompt_hidden.reshape(rows_own, chips, slice_width).transpose(1, 0, 2), "dp", 0, 0
        )
        hidden = hidden.reshape(PROMPT_COUNT, plen, slice_width)
        weights = jnp.concatenate([key_weight, value_weight], 1)

    whole_heads, one_head = (tokens, wide, jnp.float32), (tokens, HEAD_SIZE, jnp.float32)
    total, stats, *kept = attention(
        open_kernel,
        "open",
        groups,
        resp_len,
        [
            (queries, wide, 0),
            (grad_out, wide, 0),
            (keys_resp, HEAD_SIZE, 0),
            (response_value_rows, HEAD_SIZE, 0),
        ],
        [whole_heads, one_head] + [(tokens, wide, jnp.bfloat16)] * 5,
    )

    if short:
        mine, weight_terms, total, stats, kept = lax.optimization_barrier(
            (mine, weight_terms, total, stats, kept)
        )
        all_prompts = mine[:, slice_width // 2, 0].astype(jnp.int32)
        other = lax.ppermute(mine, "mp", SWAP)
        listed = take_small(all_prompts, scatter_order(chip, core))
        pairs = [project(listed[4 * k : 4 * k + 4], mine, other, weight_terms) for k in range(4)]
        prompt_rows = reduce_blocks([pair[0] for pair in pairs], [pair[1] for pair in pairs])
    else:
        terms = jnp.einsum("rtc,ck->rtk", take_blocks(hidden, all_prompts), weights, precision=HIGH)
        prompt_rows = lax.psum_scatter(
            terms.reshape(responses * plen, 2 * width), "dp", scatter_dimension=0, tiled=True
        )

    query_terms = [(x, wide, 0) for x in kept[:3]]
    upstream_terms = [(x, wide, 0) for x in kept[3:]]
    prompt_keys = (prompt_rows, HEAD_SIZE, 0)
    result, grad_scores, stats, own_k, own_v = attention(
        close_kernel,
        "close",
        groups,
        resp_len,
        query_terms
        + [(grad_out, wide, 0)]
        + upstream_terms
        + [prompt_keys, (prompt_rows, HEAD_SIZE, groups), (total, wide, 0), (stats, HEAD_SIZE, 0)],
        [whole_heads, (tokens, PER_GROUP * plen, jnp.float32), one_head]
        + [(plen, HEAD_SIZE, jnp.float32)] * 2,
    )

    def finish(stats):
        own_ins = [(keys_resp, HEAD_SIZE, 0), (response_value_rows, HEAD_SIZE, 0), prompt_keys]
        kept_ins = [(grad_scores, PER_GROUP * plen, 0), (stats, HEAD_SIZE, 0)]
        return attention(
            finish_kernel,
            "finish",
            groups,
            resp_len,
            [
                (pltpu.with_memory_space_constraint(x, pltpu.HBM), size, skip)
                for x, size, skip in query_terms + upstream_terms
            ]
            + own_ins
            + kept_ins,
            [whole_heads] + [one_head] * 2,
        )

    own = jnp.concatenate([own_k, own_v], 1)
    if short:
        place = gathered_inner(core)
        listed = take_small(all_prompts, gathered_order(chip, jnp.arange(4)))
        far = [own, permute(own, ACROSS[1])]
        ahead = permute(own, MIDDLE)
        near, third, both = [permute(own, SECOND)], [permute(own, THIRD)], []

        def group(k):
            return [far[k], near[k], third[k], both[k]]

        far[1], ahead, near[0], third[0] = lax.optimization_barrier(
            (far[1], ahead, near[0], third[0])
        )
        beyond = permute(far[1], MIDDLE)
        come = permute(ahead, OUTWARD)
        near.append(permute(far[1], SECOND))
        third.append(permute(far[1], THIRD))
        both.append(permute(near[0], THIRD))
        beyond, come, near[1] = lax.optimization_barrier((beyond, come, near[1]))
        far.append(ahead + come)
        come = permute(beyond, OUTWARD)
        near.append(permute(far[2], SECOND))
        third.append(permute(far[2], THIRD))
        both.append(permute(near[1], THIRD))
        done = hidden_part(place, group(0), weight_terms)
        come, near[2], done = lax.optimization_barrier((come, near[2], done))
        far.append(beyond + come)
        near.append(permute(far[3], SECOND))
        third.append(permute(far[3], THIRD))
        both.append(permute(near[2], THIRD))
        parts = [done]
        near[3], done = lax.optimization_barrier(
            (near[3], hidden_part(place, group(1), weight_terms))
        )
        both.append(permute(near[3], THIRD))
        parts.append(done)
        parts.append(hidden_part(place, group(2), weight_terms))
        come = [lax.ppermute(give, "mp", SWAP) for _, give in parts]
        pair = hidden_part(jnp.arange(2), [far[3], near[3]], weight_terms)
        third[3], both[3], parts, come, pair, stats_late = lax.optimization_barrier(
            (third[3], both[3], parts, come, pair, stats)
        )
        parts.append(hidden_last(place, *pair, [third[3], both[3]], weight_terms))
        come.append(lax.ppermute(parts[3][1], "mp", SWAP))
        back = lax.all_to_all(assemble(listed, [x for x, _ in parts], come), "dp", 0, 0)

        order = take_small(all_prompts, gathered_order(chip, place))
        gathered = [x for k in range(4) for x in group(k)]
        gathered, state = lax.optimization_barrier((gathered, finish(stats_late)))
        grad_w_key, grad_w_value = weight_grad(order, here, mine, other, gathered)
        back, grad_w_key, grad_w_value, state = lax.optimization_barrier(
            (back, grad_w_key, grad_w_value, state)
        )
        grad_query, grad_keys, grad_values = state
        leave = jnp.where(core == 0, back[chips // 2 :], back[: chips // 2])
        grad_hidden = turn_back(here, back, lax.ppermute(leave, "mp", SWAP))
    else:
        grad_query, grad_keys, grad_values = finish(stats)
        gathered = lax.all_gather(own, "dp", axis=0, tiled=True).reshape(responses, plen, 2 * width)
        summed = jnp.einsum(
            "rtc,rtk->ck", take_blocks(hidden, all_prompts), gathered, precision=HIGH
        )
        grad_w_key, grad_w_value = summed[:, :width], summed[:, width:]
        terms = jnp.einsum("rtk,ck->rtc", gathered, weights, precision=HIGH)
        numbers = jnp.arange(responses)
        same = all_prompts[:, None] == all_prompts[None, :]
        earlier = jnp.sum(same & (numbers[None, :] < numbers[:, None]), 1)
        hidden_terms = 0.0
        for i in range(responses // PROMPT_COUNT):
            hit = (all_prompts[None, :] == jnp.arange(PROMPT_COUNT)[:, None]) & (earlier[None, :] == i)
            place = jnp.sum(jnp.where(hit, numbers[None, :], 0), -1)
            hidden_terms = hidden_terms + take_blocks(terms, place)
        back = lax.all_to_all(hidden_terms.reshape(chips, rows_own, slice_width), "dp", 0, 0)
        back = back.transpose(1, 0, 2).reshape(rows_own, model)
        grad_hidden = lax.psum_scatter(back, "mp", scatter_dimension=1, tiled=True)
    return (
        result,
        grad_query,
        grad_keys,
        grad_values,
        grad_hidden,
        grad_w_key,
        grad_w_value,
    )


def solution(mesh):
    short = mesh.shape["dp"] == 16 and mesh.shape["mp"] == 2
    in_specs = (P("dp", None),) + (P("dp", "mp"),) * 6 + (P("dp"),) * 2
    out_specs = (P("dp", "mp"),) * 7
    return jax.shard_map(
        functools.partial(per_device, short),
        mesh=mesh,
        in_specs=in_specs,
        out_specs=out_specs,
        check_vma=False,
    )
```
